32 devices in a mesh: dp: 8 (over z, x), seq: 4 (over y, core).
Axes of the slice: x: 2, y: 2, z: 4, core: 2. Of those that a mesh axis runs over, the one named last changes fastest.
Arguments:
- residual_tiles: bfloat16 [8, 1024, 1024], P('dp', 'seq'), may hold values from -16 to 16
- picture_label_tile: int32 [8, 1024], P('dp', 'seq'), may hold values from 0 to 11, never falling along the last dimension, each value on 1 to 512 neighbouring positions
- prenorm_multiplier: float32 [1024], replicated, may hold values from 0.5 to 1.5
- triple_projector: bfloat16 [1024, 3072], P('dp'), may hold values from -0.25 to 0.25
- logit_scaling: float32 [16], replicated, may hold values from 0.3 to 30
- final_projector: bfloat16 [1024, 1024], P('dp'), may hold values from -0.1875 to 0.1875
- binarizer_projector: bfloat16 [1024, 18], replicated, may hold values from -0.1875 to 0.1875
- binarizer_offset: float32 [18], replicated, may hold values from -1 to 1
Outputs:
- mixed: bfloat16 [8, 1024, 1024], P('dp', 'seq')
- bit_codes: float32 [8, 18, 1024], P('dp', None, 'seq')
- code_entropy: float32 [18], replicated
The draws below stay inside these ranges and needn't reach their ends.
Inputs may be any that keep to these rules, and one draw needn't show every extreme that they name: `picture_label_tile`: in each pack image numbers never fall, every image number of 0 to 11 occurs, and an image has at most 512 patches.
All inputs are finite; a program needn't handle non-finite values.
Results may differ from the reference program's by a relative error of at most 0.0053.
The reference program's roundings to bfloat16 on the way count: a program that leaves them out, or rounds other values in their place, can miss the bound.
Values may be sent and summed in bfloat16 or wider, within the bound.
A program may use at most 64 MiB of HBM per device.

```python
import math
import jax
import jax.numpy as jnp
import numpy as np
from jax import lax

D = 1024
HEADS = 16
CHANNEL_COUNT = 64
BITS = 18
IMAGES = 12
SEQ = 1024
PACKS = 8


def draw_residual_tiles(key, part):
    first_key, second_key = jax.random.split(key, 2)
    pack_place = jnp.arange(PACKS, dtype=jnp.float32) / max(PACKS - 1, 1)
    token_place = jnp.arange(SEQ, dtype=jnp.float32) / max(SEQ - 1, 1)
    trend = jnp.exp(jnp.log(3.0) * pack_place)[:, None] * jnp.exp(jnp.log(2.0) * token_place)[None, :]
    rough = jnp.exp(jax.random.uniform(first_key, (PACKS, SEQ), minval=jnp.log(0.4), maxval=jnp.log(1.6)))
    base = jax.random.normal(second_key, (PACKS, SEQ, D))
    values = base * (trend * rough)[:, :, None] * 0.5
    return jnp.clip(values, -16.0, 16.0).astype(jnp.bfloat16)


def draw_triple_projector(key, part):
    first_key = jax.random.fold_in(key, 0)
    spread = D ** (-0.5)
    base = jax.random.normal(first_key, (D, 3, D)) * spread
    return jnp.clip(base.reshape(D, 3 * D), -0.25, 0.25).astype(jnp.bfloat16)


def draw_logit_scaling(key, part):
    first_key = jax.random.fold_in(key, 0)
    values = jnp.exp(jax.random.uniform(first_key, (HEADS,), minval=jnp.log(0.3), maxval=jnp.log(3.0)))
    return values.astype(jnp.float32)


def steps_of(key, extent, shards, smallest, largest):
    level, own = 1.0, jax.random.fold_in(key, 6)
    for dim, shards_of in shards:
        draws = jnp.exp(jax.random.uniform(jax.random.fold_in(own, dim), (shards_of,), jnp.float32, smallest / len(shards), largest / len(shards)))
        level = level * jnp.repeat(draws, extent[dim] // shards_of).reshape([-1 if axis == dim else 1 for axis in range(len(extent))])
    return level


def profile(amount, total, reach, lean):
    portions = [(1 << 20) // math.isqrt(rank ** lean) + 1 for rank in range(2, amount + 1)]
    surplus, holding = total - reach - (amount - 1), [1] * (amount - 1)
    while surplus > 0:
        free = [i for i in range(amount - 1) if holding[i] < reach]
        whole, budget = sum([portions[i] for i in free]), surplus
        for i in free:
            more = min(reach - holding[i], max(1, budget * portions[i] // whole), surplus)
            holding[i] = holding[i] + more
            surplus = surplus - more
    return np.array([reach] + holding)


def uneven(rng, number_of, total, limit, slope):
    if number_of == 2:
        one = jax.random.randint(rng, (), max(1, total - limit), min(limit, total - 1) + 1)
        return jnp.stack([one, total - one])
    sizes = jnp.asarray(profile(number_of, total, limit, slope), jnp.int32)
    twos = (number_of - 1) // 2
    donor, taker = sizes[1:1 + 2 * twos:2], sizes[2:2 + 2 * twos:2]
    margin = jnp.minimum(donor - 1, limit - taker)
    shifted = jax.random.randint(jax.random.fold_in(rng, 1), (twos,), 0, 1 << 20) % (margin + 1)
    sizes = sizes.at[1:1 + 2 * twos:2].set(donor - shifted).at[2:2 + 2 * twos:2].set(taker + shifted)
    return sizes[jax.random.permutation(jax.random.fold_in(rng, 2), number_of)]


def gaussian(stream_key, extent, scale, reach, cuts=(), kind=jnp.bfloat16):
    factor_of = steps_of(stream_key, extent, cuts, -0.22, 0.18) if cuts else 1.0
    result = jax.random.normal(stream_key, extent, jnp.float32) * scale * factor_of
    return jnp.minimum(jnp.maximum(result, -reach), reach).astype(kind)


def setup_inputs(seed: int = 0) -> dict:
    keys = jax.random.split(jax.random.key(seed), 9)
    return {
        "residual_tiles": draw_residual_tiles(jax.random.fold_in(keys[8], 71), 0),
        "picture_label_tile": jax.vmap(lambda own: jnp.searchsorted(jnp.cumsum(uneven(own, IMAGES, SEQ, SEQ // 2, 2)), jnp.arange(SEQ), side="right"))(jax.random.split(keys[1], PACKS)).reshape((PACKS, SEQ)).astype(jnp.int32),
        "prenorm_multiplier": jnp.clip(1.0 + 0.1 * jax.random.normal(keys[2], (D,), jnp.float32), 0.5, 1.5),
        "triple_projector": draw_triple_projector(jax.random.fold_in(keys[8], 71), 0),
        "logit_scaling": draw_logit_scaling(jax.random.fold_in(keys[8], 71), 0),
        "final_projector": gaussian(keys[5], (D, D), D ** -0.5, 0.1875, ((0, 8),)),
        "binarizer_projector": gaussian(keys[6], (D, BITS), D ** -0.5, 0.1875),
        "binarizer_offset": jnp.clip(jax.random.uniform(keys[7], (BITS,), jnp.float32, -1.0, 1.0), -1.0, 1.0),
    }


epsilon = 1e-06

def rms_scale(values):
    return lax.rsqrt(lax.optimization_barrier(jnp.mean(values * values, axis=-1, keepdims=True)) + epsilon)

def split_subspaces(combined_subspaces, scales, channel_extent):
    token_count = combined_subspaces.shape[0]
    pieces = combined_subspaces.reshape(token_count, 3, scales.shape[0], channel_extent).astype(jnp.float32)
    asking_tensor = pieces[:, 0] * rms_scale(pieces[:, 0]) * (scales[:, None] / math.sqrt(channel_extent))
    rescaled_lookups = pieces[:, 1] * rms_scale(pieces[:, 1])
    return (asking_tensor.astype(jnp.bfloat16), rescaled_lookups.astype(jnp.bfloat16), pieces[:, 2].astype(jnp.bfloat16))

def bundled_mixing_block(bundled_tokens, picture_label_column, prenorm_multiplier, triple_projector, logit_scaling, final_projector, binarizer_projector, binarizer_offset):
    wide_pack = bundled_tokens.astype(jnp.float32)
    normed = (wide_pack * rms_scale(wide_pack) * prenorm_multiplier).astype(jnp.bfloat16)
    combined_subspaces = jnp.dot(normed, triple_projector, preferred_element_type=jnp.float32).astype(jnp.bfloat16)
    asking_tensor, rescaled_lookups, surviving_contents = split_subspaces(combined_subspaces, logit_scaling, CHANNEL_COUNT)
    same_image = picture_label_column[:, None] == picture_label_column[None, :]

    def one_head(contraction_operands):
        query_head, key_head, value_head = contraction_operands
        scores = jnp.dot(query_head, key_head.T, preferred_element_type=jnp.float32)
        masked = jnp.where(same_image, scores, -1e+30)
        highest = lax.optimization_barrier(jnp.max(masked, axis=-1, keepdims=True))
        probs = jnp.where(same_image, jnp.exp(scores - highest), 0.0)
        weights = probs.astype(jnp.bfloat16)
        summed = jnp.dot(weights, value_head, preferred_element_type=jnp.float32)
        return summed / lax.optimization_barrier(jnp.sum(probs, axis=-1, keepdims=True))
    attended = lax.map(one_head, (jnp.swapaxes(asking_tensor, 0, 1), jnp.swapaxes(rescaled_lookups, 0, 1), jnp.swapaxes(surviving_contents, 0, 1)))
    attention = jnp.swapaxes(attended, 0, 1).reshape(SEQ, D).astype(jnp.bfloat16)
    hidden_state = wide_pack + jnp.dot(attention, final_projector, preferred_element_type=jnp.float32)
    mixed = hidden_state.astype(jnp.bfloat16)
    logits = jnp.dot(mixed, binarizer_projector, preferred_element_type=jnp.float32) + binarizer_offset
    return (mixed, jax.nn.sigmoid(4.0 * logits))

def reference(residual_tiles, picture_label_tile, prenorm_multiplier, triple_projector, logit_scaling, final_projector, binarizer_projector, binarizer_offset):

    def one_pack(contraction_operands):
        return bundled_mixing_block(contraction_operands[0], contraction_operands[1], prenorm_multiplier, triple_projector, logit_scaling, final_projector, binarizer_projector, binarizer_offset)
    mixed, bit_probs = lax.map(one_pack, (residual_tiles, picture_label_tile))
    marginal = lax.optimization_barrier(jnp.sum(bit_probs, axis=(0, 1))) / (PACKS * SEQ)
    code_entropy = -(marginal * jnp.log(marginal) + (1.0 - marginal) * jnp.log(1.0 - marginal))
    bit_codes = jnp.swapaxes(bit_probs - marginal, 1, 2)
    return (mixed, bit_codes, code_entropy)
```

```python
import functools
import math

import jax
import jax.numpy as jnp
from jax import lax
from jax.experimental import pallas as pl
from jax.experimental.pallas import tpu as pltpu
from jax.sharding import PartitionSpec as P

EPS = 1e-06
MESH = pl.DeviceIdType.MESH
LANES = 128
SAME = 640.0


def layer_kernel(
    cfg,
    x_ref,
    ids_ref,
    gain_ref,
    w_ref,
    scale_ref,
    wo_ref,
    bits_ref,
    off_ref,
    mixed_ref,
    codes_ref,
    ent_ref,
    wg,
    wog,
    xg,
    idg,
    normed,
    qs,
    ks,
    vs,
    ao,
    ag,
    part1,
    part2,
    local_sem,
    wz_s,
    wz_r,
    wx_s,
    wx_r,
    oz_s,
    oz_r,
    ox_s,
    ox_r,
    oy_s,
    oy_r,
    oc_s,
    oc_r,
    xy_s,
    xy_r,
    xc_s,
    xc_r,
    id_s,
    id_r,
    at_s,
    at_r,
    p1_s,
    p1_r,
    p2_s,
    p2_r,
):
    nz, nx, ny, nc = cfg["nz"], cfg["nx"], cfg["ny"], cfg["nc"]
    n = ny * nc
    ndp = nz * nx
    heads, channel = cfg["heads"], cfg["channel"]
    parts, quarters = cfg["parts"], cfg["quarters"]
    rows, width = x_ref.shape
    shard = w_ref.shape[0]
    cols = width // n
    pc = cols // parts
    sub = width // (nc * ny)
    seq_len = rows * n
    bits = bits_ref.shape[0]
    dp = lax.axis_index("dp")
    me = lax.axis_index("seq")
    z = dp // nx
    x = dp % nx
    y = me // nc
    core = me % nc

    def dp_at(zz, xx):
        return zz * nx + xx

    def seq_at(yy, cc):
        return yy * nc + cc

    def remote(src, dst, ss, rs, d, s):
        return pltpu.make_async_remote_copy(
            src_ref=src, dst_ref=dst, send_sem=ss, recv_sem=rs, device_id=(d, s), device_id_type=MESH
        )

    sends = []

    def go(make):
        make().start()
        sends.append(make)

    def arrive(slot, sem):
        remote(slot, slot, sem, sem, dp, me).wait_recv()

    def shard_rows(zz, xx):
        return pl.ds(pl.multiple_of(dp_at(zz, xx) * shard, shard), shard)

    def w_slot_of(h):
        return lambda zz, xx: wg.at[h, shard_rows(zz, xx), :]

    w_slots = [w_slot_of(h) for h in range(parts)]
    x_rows = rows // quarters

    def x_piece(member, q):
        return xg.at[member, pl.ds(q * x_rows, x_rows), :]

    def o_slot(zz, xx):
        return wog.at[core, :, shard_rows(zz, xx), :]

    def o_sub(yy, zz, xx):
        return wog.at[core, yy, shard_rows(zz, xx), :]

    lo = jnp.minimum(z, nz - 1 - z)

    def piece(i):
        near = z - (i + 1) // 2 if i % 2 else z + (i + 1) // 2
        far = jnp.where(z > nz - 1 - z, z - (i - lo), z + (i - lo))
        return jnp.where(i <= 2 * lo, near, far) if i else z

    line_sends = []

    def line_hops(slot, ss, rs, i):
        p = piece(i)
        here = slot(p, x)
        s_left, s_right = (ss.at[p], ss.at[p]) if i else (ss.at[nz], ss.at[nz + 1])
        left = remote(here, here, s_left, rs.at[p], dp_at(jnp.maximum(z - 1, 0), x), me)
        right = remote(here, here, s_right, rs.at[p], dp_at(jnp.minimum(z + 1, nz - 1), x), me)
        to_left = jnp.logical_and(p >= z, z > 0)
        to_right = jnp.logical_and(p <= z, z < nz - 1)
        return (to_left, left), (to_right, right)

    def line_start(slot, ss, rs, i):
        if nz == 1:
            return
        line_sends.append((slot, ss, rs, i))
        for wanted, hop in line_hops(slot, ss, rs, i):

            @pl.when(wanted)
            def _(hop=hop):
                hop.start()

    def cross(slot, ss, rs, i, k):
        p = piece(i)
        return remote(slot(p, x), slot(p, x), ss.at[p, k], rs.at[p, k], dp_at(z, (x + k) % nx), me)

    def across(slot, ss, rs, i):
        for k in range(1, nx):
            go(functools.partial(cross, slot, ss, rs, i, k))

    def share(src, key):
        def copy(k):
            here = src()
            return remote(here, here, oc_s.at[key, k], oc_r.at[key, k], dp, seq_at(y, (core + k) % nc))

        for k in range(1, nc):
            go(functools.partial(copy, k))

    def o_crossing(i, k, d):
        return o_sub((y - d + ny) % ny, piece(i), (x - k + nx) % nx)

    def o_over(i, k, d):
        p, s = piece(i), o_crossing(i, k, 0)
        return remote(s, s, oy_s.at[p, k, d], oy_r.at[p, k, d], dp, seq_at((y + d) % ny, core))

    def o_forward(i):
        line_start(o_slot, oz_s, oz_r, i)
        across(lambda zz, xx: o_sub(y, zz, xx), ox_s, ox_r, i)
        share(lambda: o_slot(piece(i), x), i)

    def o_line(i):
        arrive(o_slot(piece(i), x), oz_r.at[piece(i)])
        o_forward(i)

    def o_crossed(i):
        for k in range(1, nx):
            arrive(o_crossing(i, k, 0), ox_r.at[piece(i), k])
            for d in range(1, ny):
                go(functools.partial(o_over, i, k, d))
            share(functools.partial(o_crossing, i, k, 0), nz + (i * nx + k) * ny)

    def o_last(i):
        for k in range(1, nx):
            for d in range(1, ny):
                arrive(o_crossing(i, k, d), oy_r.at[piece(i), k, d])
                share(functools.partial(o_crossing, i, k, d), nz + (i * nx + k) * ny + d)

    def o_shared():
        for k in range(1, nc):
            other = (core - k + nc) % nc
            for i in range(nz):
                p = piece(i)
                s = wog.at[other, :, shard_rows(p, x), :]
                arrive(s, oc_r.at[i, k])
                for j in range(1, nx):
                    xx = (x - j + nx) % nx
                    for d in range(ny):
                        s = wog.at[other, (y - d + ny) % ny, shard_rows(p, xx), :]
                        arrive(s, oc_r.at[nz + (i * nx + j) * ny + d, k])

    own_w, own_o = [], []
    for h in range(parts):
        for part in range(3):
            own_w.append(
                pltpu.make_async_copy(
                    w_ref.at[:, pl.ds(pl.multiple_of(part * width + me * cols + h * pc, LANES), pc)],
                    wg.at[h, shard_rows(z, x), pl.ds(part * pc, pc)],
                    local_sem.at[h * 3 + part],
                )
            )
    base = 3 * parts
    own_x = pltpu.make_async_copy(x_ref, xg.at[me], local_sem.at[base])
    own_id = pltpu.make_async_copy(ids_ref, idg.at[me], local_sem.at[base + 1])
    for yy in range(ny):
        own_o.append(
            pltpu.make_async_copy(
                wo_ref.at[:, pl.ds(pl.multiple_of((core * ny + yy) * sub, LANES), sub)],
                o_sub(yy, z, x),
                local_sem.at[base + 2 + yy],
            )
        )
    for c in own_w + [own_x, own_id] + own_o:
        c.start()

    barrier = pltpu.get_barrier_semaphore()

    def greet(d, s):
        pl.semaphore_signal(barrier, inc=1, device_id=(d, s), device_id_type=MESH)

    for i in range(1, n):
        greet(dp, (me + i) % n)
    for k in range(1, nx):
        greet(dp_at(z, (x + k) % nx), me)

    @pl.when(z > 0)
    def _():
        greet(dp_at(z - 1, x), me)

    @pl.when(z < nz - 1)
    def _():
        greet(dp_at(z + 1, x), me)

    ends = jnp.where(z > 0, 1, 0) + jnp.where(z < nz - 1, 1, 0)
    pl.semaphore_wait(barrier, n - 1 + nx - 1 + ends)

    for c in own_w:
        c.wait()
    for h, slot in enumerate(w_slots):
        line_start(slot, wz_s.at[h], wz_r.at[h], 0)
        across(slot, wx_s.at[h], wx_r.at[h], 0)
    own_x.wait()
    for q in range(quarters):
        for i in range(1, ny):
            mine = x_piece(me, q)
            go(functools.partial(remote, mine, mine, xy_s.at[q, i], xy_r.at[q, i], dp, seq_at((y + i) % ny, core)))
    for k in range(1, nc):
        go(functools.partial(remote, xg.at[me], xg.at[me], xc_s.at[0, 0, k], xc_r.at[0, 0, k], dp, seq_at(y, (core + k) % nc)))
    own_id.wait()
    for i in range(1, n):
        go(functools.partial(remote, idg.at[me], idg.at[me], id_s.at[i], id_r.at[i], dp, (me + i) % n))

    gain = gain_ref[...]
    block = math.gcd(x_rows, 64)

    def norm_rows(member, q, count=1):
        start = pl.multiple_of(member * rows, rows)

        def body(b, _):
            r0 = pl.multiple_of(q * x_rows + b * block, block)
            wide = xg[member, pl.ds(r0, block), :].astype(jnp.float32)
            ms = jnp.mean(wide * wide, axis=-1, keepdims=True)
            out = (wide * lax.rsqrt(ms + EPS) * gain).astype(jnp.bfloat16)
            normed[pl.ds(start + r0, block), :] = out
            return 0

        lax.fori_loop(0, count * x_rows // block, body, 0)

    norm_rows(me, 0, quarters)
    for i in range(1, n):
        arrive(idg.at[(me - i + n) % n], id_r.at[i])
    lane_ids = lax.broadcasted_iota(jnp.int32, (rows, LANES), 1).astype(jnp.float32)
    for m in range(n):
        column = jnp.transpose(jnp.broadcast_to(idg[m].astype(jnp.float32), (LANES, rows)))
        hot = jnp.where(column == lane_ids, 1.0, 0.0)
        r = pl.ds(m * rows, rows)
        for h in range(parts):
            qs[h, r, pc:] = (hot * SAME).astype(jnp.bfloat16)
            ks[h, r, pc:] = hot.astype(jnp.bfloat16)
            vs[h, r, pc:] = jnp.ones((rows, pc), jnp.bfloat16)
    for k in range(1, nc):
        other = seq_at(y, (core - k + nc) % nc)
        arrive(xg.at[other], xc_r.at[0, 0, k])
        norm_rows(other, 0, quarters)

    def x_arrived(i, q):
        source = seq_at((y - i + ny) % ny, core)
        slot = x_piece(source, q)
        arrive(slot, xy_r.at[q, i])
        for k in range(1, nc):
            go(functools.partial(remote, slot, slot, xc_s.at[q, i, k], xc_r.at[q, i, k], dp, seq_at(y, (core + k) % nc)))
        norm_rows(source, q)

    def x_shared(i, q):
        for k in range(1, nc):
            other = seq_at((y - i + ny) % ny, (core - k + nc) % nc)
            arrive(x_piece(other, q), xc_r.at[q, i, k])
            norm_rows(other, q)

    def w_cross(i, h):
        across(w_slots[h], wx_s.at[h], wx_r.at[h], i)

    def w_arrived(i, h):
        arrive(w_slots[h](piece(i), x), wz_r.at[h, piece(i)])
        line_start(w_slots[h], wz_s.at[h], wz_r.at[h], i)
        if h == 0:
            w_cross(i, 0)
            for hh in range(1, parts):
                if i > 1:
                    w_cross(i - 1, hh)
        elif i == nz - 1:
            w_cross(i, h)

    events = []
    for i in range(1, nz):
        for h in range(parts):
            events.append((((i - 1) * parts + h + 1) * shard * 3 * pc, 0, i, h))
    for i in range(1, ny):
        for q in range(quarters):
            events.append((((i - 1) * quarters + q + 1) * x_rows * width, 1, i, q))
    waiting = []
    for _, stream, i, j in sorted(events):
        if stream == 0:
            w_arrived(i, j)
        else:
            x_arrived(i, j)
            waiting.append((i, j))
            if len(waiting) > 1:
                x_shared(*waiting.pop(0))
    for c in own_o:
        c.wait()
    o_forward(0)
    for late in waiting:
        x_shared(*late)

    row_block = 256
    blocks = seq_len // row_block

    def group_of(shape, dim):
        return lax.div(lax.broadcasted_iota(jnp.int32, shape, dim), jnp.int32(channel))

    pair = (2 * pc, 2 * pc)
    same_head = jnp.where(group_of(pair, 0) == group_of(pair, 1), 1.0, 0.0).astype(jnp.bfloat16)
    part_heads = pc // channel

    def project(h):
        scale_row = jnp.ones((1, 2 * pc), jnp.float32)
        for g in range(part_heads):
            value = scale_ref[me * heads + h * part_heads + g] / math.sqrt(channel)
            scale_row = jnp.where(group_of((1, 2 * pc), 1) == g, value, scale_row)
        for i in range(nz):
            for k in range(1, nx):
                arrive(w_slots[h](piece(i), (x - k + nx) % nx), wx_r.at[h, piece(i), k])

        def body(b, _):
            r = pl.ds(pl.multiple_of(b * row_block, row_block), row_block)
            joined = jnp.dot(normed[r, :], wg[h], preferred_element_type=jnp.float32).astype(jnp.bfloat16)
            qk = joined[:, : 2 * pc].astype(jnp.float32)
            square = qk * qk
            high = square.astype(jnp.bfloat16)
            low = (square - high.astype(jnp.float32)).astype(jnp.bfloat16)
            total = jnp.dot(high, same_head, preferred_element_type=jnp.float32) + jnp.dot(
                low, same_head, preferred_element_type=jnp.float32
            )
            qk = (qk * lax.rsqrt(total / channel + EPS) * scale_row).astype(jnp.bfloat16)
            qs[h, r, :pc] = qk[:, :pc]
            ks[h, r, :pc] = qk[:, pc:]
            vs[h, r, :pc] = joined[:, 2 * pc :]
            return 0

        lax.fori_loop(0, blocks, body, 0)

    q_block = cfg["q_block"]
    lane_head = group_of((q_block, pc), 1)

    def stage_target(t, sign):
        dy = (t // nc + 1) % ny
        dc = (t + 1) % nc
        if sign > 0:
            return seq_at((y + dy) % ny, (core + dc) % nc)
        return seq_at((y - dy + ny) % ny, (core - dc + nc) % nc)

    def a2a(h, t):
        j = stage_target(t, 1)
        return remote(ao.at[h, j], ag.at[h, me], at_s.at[h, t], at_r.at[h, t], dp, j)

    def attend(h, chores):
        def stage(t, _):
            j = stage_target(t, 1)
            for part in range(rows // q_block):
                r = pl.ds(pl.multiple_of(j * rows + part * q_block, q_block), q_block)
                qb = qs[h, r, :]
                out = jnp.zeros((q_block, pc), jnp.float32)
                for g in range(part_heads):
                    mine = lane_head == g
                    qh = jnp.concatenate([jnp.where(mine, qb[:, :pc], jnp.zeros_like(qb[:, :pc])), qb[:, pc:]], axis=1)
                    s = lax.dot_general(qh, ks[h], (((1,), (1,)), ((), ())), preferred_element_type=jnp.float32)
                    p = jnp.exp(s - jnp.max(s, axis=-1, keepdims=True))
                    o = jnp.dot(p.astype(jnp.bfloat16), vs[h], preferred_element_type=jnp.float32)
                    out = jnp.where(mine, o[:, :pc] / o[:, pc:], out)
                ao[h, j, pl.ds(part * q_block, q_block), :] = out.astype(jnp.bfloat16)

            @pl.when(t < n - 1)
            def _():
                a2a(h, t).start()

            for at in sorted(set(chores)):

                @pl.when(t == at)
                def _(at=at):
                    for c in chores[at]:
                        c()

            return 0

        lax.fori_loop(0, n, stage, 0)

    todo = []
    for i in range(1, nz + 2):
        if i < nz:
            todo.append(functools.partial(o_line, i))
        if 0 <= i - 2 < nz:
            todo.append(functools.partial(o_crossed, i - 2))
        if 0 <= i - 3 < nz:
            todo.append(functools.partial(o_last, i - 3))
    todo += [functools.partial(o_last, i) for i in range(max(0, nz - 1), nz)]

    for h in range(parts):
        project(h)
        chores = {}
        if h == parts - 1:
            for t in range(n):
                chores[t] = [todo.pop(0) for _ in range(min(len(todo), 1))]
        else:
            chores[n - 1] = [todo.pop(0)]
        attend(h, chores)
    for c in todo:
        c()
    o_shared()

    for h in range(parts):
        for t in range(n - 1):
            arrive(ag.at[h, stage_target(t, -1)], at_r.at[h, t])
        ag[h, me] = ao[h, me]

    attention = jnp.concatenate([ag[h, m] for m in range(n) for h in range(parts)], axis=1)
    for g in range(nc * ny):
        lanes = slice(g * sub, (g + 1) * sub)
        prod = jnp.dot(attention, wog[g // ny, g % ny], preferred_element_type=jnp.float32)
        mixed_ref[:, lanes] = (xg[me, :, lanes].astype(jnp.float32) + prod).astype(jnp.bfloat16)

    logits = lax.dot_general(
        bits_ref[...], mixed_ref[...], (((1,), (1,)), ((), ())), preferred_element_type=jnp.float32
    )
    eye = lax.broadcasted_iota(jnp.int32, (bits, bits), 0) == lax.broadcasted_iota(
        jnp.int32, (bits, bits), 1
    )
    offset = jnp.sum(jnp.where(eye, off_ref[...], 0.0), axis=1, keepdims=True)
    probs = jax.nn.sigmoid(4.0 * (logits + offset))
    lanes_eye = lax.broadcasted_iota(jnp.int32, (bits, LANES), 0) == lax.broadcasted_iota(
        jnp.int32, (bits, LANES), 1
    )
    own_sums = jnp.sum(probs, axis=1, keepdims=True)
    part1[me, :, :] = jnp.sum(jnp.where(lanes_eye, own_sums, 0.0), axis=0, keepdims=True)
    for i in range(1, n):
        go(functools.partial(remote, part1.at[me], part1.at[me], p1_s.at[i], p1_r.at[i], dp, (me + i) % n))
    for i in range(1, n):
        arrive(part1.at[(me - i + n) % n], p1_r.at[i])
    pack = part1[0]
    for m in range(1, n):
        pack = pack + part1[m]
    part2[dp, :, :] = pack
    for i in range(1, ndp):
        go(functools.partial(remote, part2.at[dp], part2.at[dp], p2_s.at[i], p2_r.at[i], (dp + i) % ndp, me))
    for i in range(1, ndp):
        arrive(part2.at[(dp - i + ndp) % ndp], p2_r.at[i])
    total = part2[0]
    for m in range(1, ndp):
        total = total + part2[m]
    marginal = total / (seq_len * ndp)
    line = marginal[:, :bits]
    ent_ref[...] = -(line * jnp.log(line) + (1.0 - line) * jnp.log(1.0 - line))
    codes = probs - jnp.sum(jnp.where(lanes_eye, marginal, 0.0), axis=1, keepdims=True)
    for b in range(bits):
        codes_ref[b] = codes[b : b + 1, :]

    for make in sends:
        make().wait_send()
    for h in range(parts):
        for t in range(n - 1):
            a2a(h, t).wait_send()
    for hops in line_sends:
        for wanted, hop in line_hops(*hops):

            @pl.when(wanted)
            def _(hop=hop):
                hop.wait_send()


def on_device(
    cfg,
    residual_tiles,
    picture_label_tile,
    prenorm_multiplier,
    triple_projector,
    logit_scaling,
    final_projector,
    binarizer_projector,
    binarizer_offset,
):
    nz, nx, ny, nc = cfg["nz"], cfg["nx"], cfg["ny"], cfg["nc"]
    n, ndp = ny * nc, nz * nx
    _, rows, width = residual_tiles.shape
    heads_all = logit_scaling.shape[0]
    bits = binarizer_projector.shape[1]
    cols = width // n
    shard = triple_projector.shape[0]
    seq_len = rows * n
    parts = cols // LANES if cols % LANES == 0 else 1
    pc, sub = cols // parts, width // (nc * ny)
    quarters = 4 if rows % 128 == 0 else 1
    cfg = dict(
        cfg,
        heads=heads_all // n,
        channel=width // heads_all,
        q_block=min(256, rows),
        parts=parts,
        quarters=quarters,
    )
    dma = pltpu.SemaphoreType.DMA
    vmem, hbm = pl.BlockSpec(memory_space=pltpu.VMEM), pl.BlockSpec(memory_space=pl.ANY)
    smem = pl.BlockSpec(memory_space=pltpu.SMEM)
    bf16, f32 = jnp.bfloat16, jnp.float32
    keys = nz + nz * nx * ny + nx * ny
    mixed, codes, ent = pl.pallas_call(
        functools.partial(layer_kernel, cfg),
        out_shape=(
            pltpu.VMEM((rows, width), bf16),
            pltpu.VMEM((bits, 1, rows), f32),
            pltpu.VMEM((1, bits), f32),
        ),
        in_specs=[hbm, vmem, vmem, hbm, smem, hbm, vmem, vmem],
        out_specs=(vmem, vmem, vmem),
        scratch_shapes=[
            pltpu.VMEM((parts, width, 3 * pc), bf16),
            pltpu.VMEM((nc, ny, width, sub), bf16),
            pltpu.VMEM((n, rows, width), bf16),
            pltpu.VMEM((n, 1, rows), jnp.int32),
            pltpu.VMEM((seq_len, width), bf16),
            pltpu.VMEM((parts, seq_len, pc + LANES), bf16),
            pltpu.VMEM((parts, seq_len, pc + LANES), bf16),
            pltpu.VMEM((parts, seq_len, 2 * pc), bf16),
            pltpu.VMEM((parts, n, rows, pc), bf16),
            pltpu.VMEM((parts, n, rows, pc), bf16),
            pltpu.VMEM((n, 1, LANES), f32),
            pltpu.VMEM((ndp, 1, LANES), f32),
            dma((3 * parts + 2 + ny,)),
            dma((parts, nz + 2)),
            dma((parts, nz)),
            dma((parts, nz, nx)),
            dma((parts, nz, nx)),
            dma((nz + 2,)),
            dma((nz,)),
            dma((nz, nx)),
            dma((nz, nx)),
            dma((nz, nx, ny)),
            dma((nz, nx, ny)),
            dma((keys, nc)),
            dma((keys, nc)),
            dma((quarters, ny)),
            dma((quarters, ny)),
            dma((quarters, ny, nc)),
            dma((quarters, ny, nc)),
            dma((n,)),
            dma((n,)),
            dma((parts, n)),
            dma((parts, n)),
            dma((n,)),
            dma((n,)),
            dma((ndp,)),
            dma((ndp,)),
        ],
        compiler_params=pltpu.CompilerParams(
            collective_id=0, has_side_effects=True, vmem_limit_bytes=56 * 1024 * 1024
        ),
        name="layer",
    )(
        residual_tiles[0],
        picture_label_tile,
        prenorm_multiplier[None],
        triple_projector,
        logit_scaling,
        final_projector,
        binarizer_projector.T,
        binarizer_offset[None],
    )
    return mixed[None], jnp.swapaxes(codes, 0, 1), ent[0]


def solution(mesh):
    ndp, n = mesh.shape["dp"], mesh.shape["seq"]
    nx = math.isqrt(ndp // 2)
    if nx < 1 or ndp % nx:
        nx = 1
    nc = 2 if n % 2 == 0 else 1
    cfg = {"nz": ndp // nx, "nx": nx, "ny": n // nc, "nc": nc}
    return jax.shard_map(
        functools.partial(on_device, cfg),
        mesh=mesh,
        in_specs=(
            P("dp", "seq", None),
            P("dp", "seq"),
            P(),
            P("dp", None),
            P(),
            P("dp", None),
            P(),
            P(),
        ),
        out_specs=(P("dp", "seq", None), P("dp", None, "seq"), P()),
        check_vma=False,
    )
```

```python
import functools
import math

import jax
import jax.numpy as jnp
from jax import lax
from jax.experimental import pallas as pl
from jax.experimental.pallas import tpu as pltpu
from jax.sharding import PartitionSpec as P

EPS = 1e-06
MESH = pl.DeviceIdType.MESH
LANES = 128
SAME = 640.0


def layer_kernel(
    cfg,
    x_ref,
    ids_ref,
    gain_hbm,
    w_ref,
    scale_hbm,
    wo_ref,
    bits_hbm,
    off_hbm,
    mixed_ref,
    codes_ref,
    ent_ref,
    wg,
    wog,
    xg,
    idg,
    normed,
    qs,
    ks,
    vs,
    ao,
    ag,
    stats,
    gain_ref,
    scale_ref,
    bits_ref,
    off_ref,
    local_sem,
    wz_s,
    wz_r,
    wx_s,
    wx_r,
    oz_s,
    oz_r,
    ox_s,
    ox_r,
    oy_s,
    oy_r,
    oc_s,
    oc_r,
    xy_s,
    xy_r,
    xc_s,
    own_r,
    xc_r,
    id_s,
    id_r,
    at_s,
    at_r,
    st_s,
    st_r,
):
    nz, nx, ny, nc = cfg["nz"], cfg["nx"], cfg["ny"], cfg["nc"]
    n = ny * nc
    ndp = nz * nx
    heads, channel = cfg["heads"], cfg["channel"]
    parts, quarters = cfg["parts"], cfg["quarters"]
    rows, width = x_ref.shape
    shard = w_ref.shape[0]
    cols = width // n
    pc = cols // parts
    sub = width // (nc * ny)
    seq_len = rows * n
    bits = bits_ref.shape[0]
    dp = lax.axis_index("dp")
    me = lax.axis_index("seq")
    z = dp // nx
    x = dp % nx
    y = me // nc
    core = me % nc

    def dp_at(zz, xx):
        return zz * nx + xx

    def seq_at(yy, cc):
        return yy * nc + cc

    def remote(src, dst, ss, rs, d, s):
        return pltpu.make_async_remote_copy(
            src_ref=src, dst_ref=dst, send_sem=ss, recv_sem=rs, device_id=(d, s), device_id_type=MESH
        )

    def arrive(slot, sem):
        remote(slot, slot, sem, sem, dp, me).wait_recv()

    def left(slot, sem):
        remote(slot, slot, sem, sem, dp, me).wait_send()

    def shard_rows(zz, xx):
        return pl.ds(pl.multiple_of(dp_at(zz, xx) * shard, shard), shard)

    def w_slot_of(h):
        return lambda zz, xx: wg.at[h, shard_rows(zz, xx), :]

    w_slots = [w_slot_of(h) for h in range(parts)]
    x_rows = rows // quarters

    def x_piece(member, q):
        return xg.at[member, pl.ds(q * x_rows, x_rows), :]

    def o_slot(zz, xx):
        return wog.at[core, :, shard_rows(zz, xx), :]

    def o_sub(yy, zz, xx):
        return wog.at[core, yy, shard_rows(zz, xx), :]

    lo = jnp.minimum(z, nz - 1 - z)

    def piece(i):
        near = z - (i + 1) // 2 if i % 2 else z + (i + 1) // 2
        far = jnp.where(z > nz - 1 - z, z - (i - lo), z + (i - lo))
        return jnp.where(i <= 2 * lo, near, far) if i else z

    def line_start(slot, ss, rs, i, when=True):
        if nz == 1:
            return
        p = piece(i)
        here = slot(p, x)
        to_left = remote(here, here, ss.at[0], rs.at[p], dp_at(jnp.maximum(z - 1, 0), x), me)
        to_right = remote(here, here, ss.at[1], rs.at[p], dp_at(jnp.minimum(z + 1, nz - 1), x), me)
        for wanted, hop in (
            (jnp.logical_and(p >= z, z > 0), to_left),
            (jnp.logical_and(p <= z, z < nz - 1), to_right),
        ):

            @pl.when(wanted if when is True else jnp.logical_and(wanted, when))
            def _(hop=hop):
                hop.start()

    def line_left(block, ss):
        for zz in range(nz if nz > 1 else 0):

            @pl.when(z == zz)
            def _(zz=zz):
                if zz > 0:
                    left(block(nz - zz), ss.at[0])
                if zz < nz - 1:
                    left(block(zz + 1), ss.at[1])

    def across(slot, ss, rs, i):
        p = piece(i)
        for k in range(1, nx):
            remote(slot(p, x), slot(p, x), ss, rs(k), dp_at(z, (x + k) % nx), me).start()

    def share(here):
        for k in range(1, nc):
            remote(here, here, oc_s.at[k], oc_r.at[k], dp, seq_at(y, (core + k) % nc)).start()

    def whole(i):
        return i >= nz - 2 or ny == 1

    def o_crossing(i, k, d):
        p, xx = piece(i), (x - k + nx) % nx
        return o_slot(p, xx) if whole(i) else o_sub((y - d + ny) % ny, p, xx)

    def o_line_start(i, when=True):
        line_start(o_slot, oz_s, oz_r, i, when)

    def o_cross(i):
        slot = o_slot if whole(i) else lambda zz, xx: o_sub(y, zz, xx)
        across(slot, ox_s.at[int(whole(i))], lambda k: ox_r.at[i, k], i)

    def o_line(i):
        p = piece(i)
        arrive(o_slot(p, x), oz_r.at[p])
        o_line_start(i)
        o_cross(i)
        share(o_slot(p, x))

    def o_crossed(i):
        for k in range(1, nx):
            here = o_crossing(i, k, 0)
            arrive(here, ox_r.at[i, k])
            if not whole(i):
                for d in range(1, ny):
                    remote(
                        here, here, oy_s.at[d], oy_r.at[i, k, d], dp, seq_at((y + d) % ny, core)
                    ).start()
            share(here)

    def o_last(i):
        for k in range(1, nx):
            for d in range(1, 1 if whole(i) else ny):
                arrive(o_crossing(i, k, d), oy_r.at[i, k, d])
                share(o_crossing(i, k, d))

    def o_shared():
        for k in range(1, nc):
            arrive(wog.at[(core - k + nc) % nc], oc_r.at[k])

    own_w, own_o = [], []
    for h in range(parts):
        for part in range(3):
            own_w.append(
                pltpu.make_async_copy(
                    w_ref.at[:, pl.ds(pl.multiple_of(part * width + me * cols + h * pc, LANES), pc)],
                    wg.at[h, shard_rows(z, x), pl.ds(part * pc, pc)],
                    local_sem.at[0],
                )
            )
    own_x = pltpu.make_async_copy(x_ref, xg.at[me], local_sem.at[1])
    own_id = pltpu.make_async_copy(ids_ref, idg.at[me], local_sem.at[2])
    for yy in range(ny):
        own_o.append(
            pltpu.make_async_copy(
                wo_ref.at[:, pl.ds(pl.multiple_of((core * ny + yy) * sub, LANES), sub)],
                o_sub(yy, z, x),
                local_sem.at[3],
            )
        )
    own_small = [
        pltpu.make_async_copy(src, dst, local_sem.at[4 + i])
        for i, (src, dst) in enumerate(
            ((gain_hbm, gain_ref), (scale_hbm, scale_ref), (bits_hbm, bits_ref), (off_hbm, off_ref))
        )
    ]
    for c in own_w + [own_id, own_x] + own_small + own_o:
        c.start()

    barrier = pltpu.get_barrier_semaphore()

    def greet(d, s):
        pl.semaphore_signal(barrier, inc=1, device_id=(d, s), device_id_type=MESH)

    for i in range(1, n):
        greet(dp, (me + i) % n)
    for k in range(1, nx):
        greet(dp_at(z, (x + k) % nx), me)

    @pl.when(z > 0)
    def _():
        greet(dp_at(z - 1, x), me)

    @pl.when(z < nz - 1)
    def _():
        greet(dp_at(z + 1, x), me)

    ends = jnp.where(z > 0, 1, 0) + jnp.where(z < nz - 1, 1, 0)
    pl.semaphore_wait(barrier, n - 1 + nx - 1 + ends)

    own_block = wg.at[:, shard_rows(z, x), :]
    pltpu.make_async_copy(own_block, own_block, local_sem.at[0]).wait()

    def w_forward(i, h):
        line_start(w_slots[h], wz_s, wz_r.at[h], i)
        across(w_slots[h], wx_s.at[h], lambda k: wx_r.at[h], i)

    for h in range(parts):
        w_forward(0, h)
    own_id.wait()
    for i in range(1, n):
        remote(idg.at[me], idg.at[me], id_s, id_r, dp, (me + i) % n).start()
    own_x.wait()
    for q in range(quarters):
        for i in range(1, ny):
            mine = x_piece(me, q)
            remote(mine, mine, xy_s.at[i], xy_r.at[q, i], dp, seq_at((y + i) % ny, core)).start()
    for k in range(1, nc):
        remote(xg.at[me], xg.at[me], xc_s.at[k], own_r.at[k], dp, seq_at(y, (core + k) % nc)).start()

    for c in own_small:
        c.wait()
    own_block = o_slot(z, x)
    pltpu.make_async_copy(own_block, own_block, local_sem.at[3]).wait()
    o_line_start(0, lo == 0)

    gain = gain_ref[...]
    block = math.gcd(x_rows, 64)

    def norm_rows(member, q, count=1):
        start = pl.multiple_of(member * rows, rows)

        def body(b, _):
            r0 = pl.multiple_of(q * x_rows + b * block, block)
            wide = xg[member, pl.ds(r0, block), :].astype(jnp.float32)
            ms = jnp.mean(wide * wide, axis=-1, keepdims=True)
            out = (wide * lax.rsqrt(ms + EPS) * gain).astype(jnp.bfloat16)
            normed[pl.ds(start + r0, block), :] = out
            return 0

        lax.fori_loop(0, count * x_rows // block, body, 0)

    norm_rows(me, 0, quarters)
    arrive(idg.at[pl.ds(0, n - 1)], id_r)
    lane_ids = lax.broadcasted_iota(jnp.int32, (rows, LANES), 1).astype(jnp.float32)
    for m in range(n):
        column = jnp.transpose(jnp.broadcast_to(idg[m].astype(jnp.float32), (LANES, rows)))
        hot = jnp.where(column == lane_ids, 1.0, 0.0)
        r = pl.ds(m * rows, rows)
        for h in range(parts):
            qs[h, r, pc:] = (hot * SAME).astype(jnp.bfloat16)
            ks[h, r, pc:] = hot.astype(jnp.bfloat16)
            vs[h, r, pc:] = jnp.ones((rows, pc), jnp.bfloat16)
    for k in range(1, nc):
        other = seq_at(y, (core - k + nc) % nc)
        arrive(xg.at[other], own_r.at[k])
        norm_rows(other, 0, quarters)

    def x_arrived(i, q):
        source = seq_at((y - i + ny) % ny, core)
        slot = x_piece(source, q)
        arrive(slot, xy_r.at[q, i])
        for k in range(1, nc):
            remote(slot, slot, xc_s.at[k], xc_r.at[q, i - 1, k], dp, seq_at(y, (core + k) % nc)).start()
        norm_rows(source, q)

    def x_shared(i, q):
        for k in range(1, nc):
            other = seq_at((y - i + ny) % ny, (core - k + nc) % nc)
            arrive(x_piece(other, q), xc_r.at[q, i - 1, k])
            norm_rows(other, q)

    def w_arrived(i, h):
        arrive(w_slots[h](piece(i), x), wz_r.at[h, piece(i)])
        w_forward(i, h)

    events = []
    for i in range(1, nz):
        for h in range(parts):
            events.append((((i - 1) * parts + h + 1) * shard * 3 * pc, 0, i, h))
    for i in range(1, ny):
        for q in range(quarters):
            events.append((((i - 1) * quarters + q + 1) * x_rows * width, 1, i, q))
    waiting = []
    for _, stream, i, j in sorted(events):
        if stream == 0:
            w_arrived(i, j)
        else:
            x_arrived(i, j)
            waiting.append((i, j))
            if len(waiting) > 1:
                x_shared(*waiting.pop(0))
    o_line_start(0, lo > 0)
    o_cross(0)
    share(o_slot(z, x))
    for late in waiting:
        x_shared(*late)

    row_block = 256
    blocks = seq_len // row_block

    def group_of(shape, dim):
        return lax.div(lax.broadcasted_iota(jnp.int32, shape, dim), jnp.int32(channel))

    pair = (2 * pc, 2 * pc)
    same_head = jnp.where(group_of(pair, 0) == group_of(pair, 1), 1.0, 0.0).astype(jnp.bfloat16)
    part_heads = pc // channel

    def project(h):
        scale_row = jnp.ones((1, 2 * pc), jnp.float32)
        for g in range(part_heads):
            value = scale_ref[me * heads + h * part_heads + g] / math.sqrt(channel)
            scale_row = jnp.where(group_of((1, 2 * pc), 1) == g, value, scale_row)
        if nx > 1:
            arrive(wg.at[h, pl.ds(0, nz * (nx - 1) * shard), :], wx_r.at[h])

        for b in range(blocks):
            r = pl.ds(b * row_block, row_block)
            joined = jnp.dot(normed[r, :], wg[h], preferred_element_type=jnp.float32).astype(jnp.bfloat16)
            qk = joined[:, : 2 * pc].astype(jnp.float32)
            square = qk * qk
            high = square.astype(jnp.bfloat16)
            low = (square - high.astype(jnp.float32)).astype(jnp.bfloat16)
            total = jnp.dot(high, same_head, preferred_element_type=jnp.float32) + jnp.dot(
                low, same_head, preferred_element_type=jnp.float32
            )
            qk = (qk * lax.rsqrt(total / channel + EPS) * scale_row).astype(jnp.bfloat16)
            qs[h, r, :pc] = qk[:, :pc]
            ks[h, r, :pc] = qk[:, pc:]
            vs[h, r, :pc] = joined[:, 2 * pc :]

    q_block = cfg["q_block"]
    lane_head = group_of((q_block, pc), 1)

    def stage_target(t, sign):
        dy = (t // nc + 1) % ny
        dc = (t + 1) % nc
        if sign > 0:
            return seq_at((y + dy) % ny, (core + dc) % nc)
        return seq_at((y - dy + ny) % ny, (core - dc + nc) % nc)

    def a2a(h, t):
        j = stage_target(t, 1)
        return remote(ao.at[h, j], ag.at[h, me], at_s.at[h], at_r.at[h], dp, j)

    def attend(h, stages):
        for t in stages:
            j = stage_target(t, 1)
            for part in range(rows // q_block):
                r = pl.ds(pl.multiple_of(j * rows + part * q_block, q_block), q_block)
                qb = qs[h, r, :]
                out = jnp.zeros((q_block, pc), jnp.float32)
                for g in range(part_heads):
                    mine = lane_head == g
                    qh = jnp.concatenate([jnp.where(mine, qb[:, :pc], jnp.zeros_like(qb[:, :pc])), qb[:, pc:]], axis=1)
                    s = lax.dot_general(qh, ks[h], (((1,), (1,)), ((), ())), preferred_element_type=jnp.float32)
                    p = jnp.exp(s - jnp.max(s, axis=-1, keepdims=True))
                    o = jnp.dot(p.astype(jnp.bfloat16), vs[h], preferred_element_type=jnp.float32)
                    out = jnp.where(mine, o[:, :pc] / o[:, pc:], out)
                ao[h, j, pl.ds(part * q_block, q_block), :] = out.astype(jnp.bfloat16)
        for t in stages:
            if t < n - 1:
                a2a(h, t).start()

    for i in range(1, nz - 1):
        o_line(i)
    for h in range(parts):
        project(h)
        if h < parts - 1:
            attend(h, range(n))
            if h == 0 and nz > 1:
                o_line(nz - 1)
        else:
            o_crossed(0)
            attend(h, range(n // 2))
            if parts == 1 and nz > 1:
                o_line(nz - 1)
            if nz > 1:
                o_crossed(1)
            attend(h, range(n // 2, n))
    for i in range(2, nz):
        o_last(i - 2)
        o_crossed(i)
    for i in range(max(0, nz - 2), nz):
        o_last(i)
    o_shared()

    for h in range(parts):
        arrive(ag.at[h, pl.ds(0, n - 1)], at_r.at[h])
        ag[h, me] = ao[h, me]

    attention = jnp.concatenate([ag[h, m] for m in range(n) for h in range(parts)], axis=1)
    for g in range(nc * ny):
        lanes = slice(g * sub, (g + 1) * sub)
        prod = jnp.dot(attention, wog[g // ny, g % ny], preferred_element_type=jnp.float32)
        mixed_ref[:, lanes] = (xg[me, :, lanes].astype(jnp.float32) + prod).astype(jnp.bfloat16)

    logits = lax.dot_general(
        bits_ref[...], mixed_ref[...], (((1,), (1,)), ((), ())), preferred_element_type=jnp.float32
    )
    eye = lax.broadcasted_iota(jnp.int32, (bits, bits), 0) == lax.broadcasted_iota(
        jnp.int32, (bits, bits), 1
    )
    offset = jnp.sum(jnp.where(eye, off_ref[...], 0.0), axis=1, keepdims=True)
    probs = jax.nn.sigmoid(4.0 * (logits + offset))
    lanes_eye = lax.broadcasted_iota(jnp.int32, (bits, LANES), 0) == lax.broadcasted_iota(
        jnp.int32, (bits, LANES), 1
    )
    own_sums = jnp.sum(probs, axis=1, keepdims=True)
    count = n * ndp
    mine = dp * n + me
    stats[mine, :, :] = jnp.sum(jnp.where(lanes_eye, own_sums, 0.0), axis=0, keepdims=True)

    def tell(i, _):
        t = (mine + i) % count
        remote(stats.at[mine], stats.at[mine], st_s, st_r, t // n, t % n).start()
        return 0

    lax.fori_loop(1, count, tell, 0)
    others = stats.at[pl.ds(0, count - 1)]
    arrive(others, st_r)
    total = jnp.sum(stats[...], axis=0)
    marginal = total / (seq_len * ndp)
    line = marginal[:, :bits]
    ent_ref[...] = -(line * jnp.log(line) + (1.0 - line) * jnp.log(1.0 - line))
    codes = probs - jnp.sum(jnp.where(lanes_eye, marginal, 0.0), axis=1, keepdims=True)
    for b in range(bits):
        codes_ref[b] = codes[b : b + 1, :]

    left(others, st_s)
    line_left(lambda m: wg.at[:, pl.ds(0, m * shard), :], wz_s)
    line_left(lambda m: wog.at[0, :, pl.ds(0, m * shard), :], oz_s)
    halves = [i for i in range(nz) if not whole(i)]
    if nx > 1:
        for h in range(parts):
            left(wg.at[h, pl.ds(0, nz * (nx - 1) * shard), :], wx_s.at[h])
        if halves:
            block = wog.at[0, 0, pl.ds(0, len(halves) * (nx - 1) * shard), :]
            left(block, ox_s.at[0])
            for d in range(1, ny):
                left(block, oy_s.at[d])
        if len(halves) < nz:
            left(wog.at[0, :, pl.ds(0, (nz - len(halves)) * (nx - 1) * shard), :], ox_s.at[1])
    for k in range(1, nc):
        left(wog.at[core], oc_s.at[k])
        left(xg.at[pl.ds(0, ny)], xc_s.at[k])
    for i in range(1, ny):
        left(xg.at[me], xy_s.at[i])
    left(idg.at[pl.ds(0, n - 1)], id_s)
    for h in range(parts):
        left(ag.at[h, pl.ds(0, n - 1)], at_s.at[h])


def put_kernel(mixed_ref, codes_ref, ent_ref, mixed_out, codes_out, ent_out, sems):
    pairs = ((mixed_ref, mixed_out), (codes_ref, codes_out), (ent_ref, ent_out))
    copies = [pltpu.make_async_copy(src, dst, sems.at[i]) for i, (src, dst) in enumerate(pairs)]
    for c in copies:
        c.start()
    for c in copies:
        c.wait()


def on_device(
    cfg,
    residual_tiles,
    picture_label_tile,
    prenorm_multiplier,
    triple_projector,
    logit_scaling,
    final_projector,
    binarizer_projector,
    binarizer_offset,
):
    nz, nx, ny, nc = cfg["nz"], cfg["nx"], cfg["ny"], cfg["nc"]
    n, ndp = ny * nc, nz * nx
    _, rows, width = residual_tiles.shape
    heads_all = logit_scaling.shape[0]
    bits = binarizer_projector.shape[1]
    cols = width // n
    shard = triple_projector.shape[0]
    seq_len = rows * n
    parts = cols // LANES if cols % LANES == 0 else 1
    pc, sub = cols // parts, width // (nc * ny)
    quarters = 4 if rows % 128 == 0 else 1
    cfg = dict(
        cfg,
        heads=heads_all // n,
        channel=width // heads_all,
        q_block=min(256, rows),
        parts=parts,
        quarters=quarters,
    )
    dma = pltpu.SemaphoreType.DMA
    vmem, hbm = pl.BlockSpec(memory_space=pltpu.VMEM), pl.BlockSpec(memory_space=pl.ANY)
    bf16, f32 = jnp.bfloat16, jnp.float32
    mixed, codes, ent = pl.pallas_call(
        functools.partial(layer_kernel, cfg),
        out_shape=(
            pltpu.VMEM((rows, width), bf16),
            pltpu.VMEM((bits, 1, rows), f32),
            pltpu.VMEM((1, bits), f32),
        ),
        in_specs=[hbm] * 8,
        out_specs=(vmem, vmem, vmem),
        scratch_shapes=[
            pltpu.VMEM((parts, width, 3 * pc), bf16),
            pltpu.VMEM((nc, ny, width, sub), bf16),
            pltpu.VMEM((n, rows, width), bf16),
            pltpu.VMEM((n, 1, rows), jnp.int32),
            pltpu.VMEM((seq_len, width), bf16),
            pltpu.VMEM((parts, seq_len, pc + LANES), bf16),
            pltpu.VMEM((parts, seq_len, pc + LANES), bf16),
            pltpu.VMEM((parts, seq_len, 2 * pc), bf16),
            pltpu.VMEM((parts, n, rows, pc), bf16),
            pltpu.VMEM((parts, n, rows, pc), bf16),
            pltpu.VMEM((n * ndp, 1, LANES), f32),
            pltpu.VMEM((1, width), f32),
            pltpu.SMEM((heads_all,), f32),
            pltpu.VMEM((bits, width), bf16),
            pltpu.VMEM((1, bits), f32),
            dma((8,)),
            dma((2,)),
            dma((parts, nz)),
            dma((parts,)),
            dma((parts,)),
            dma((2,)),
            dma((nz,)),
            dma((2,)),
            dma((nz, nx)),
            dma((ny,)),
            dma((max(1, nz - 2), nx, ny)),
            dma((nc,)),
            dma((nc,)),
            dma((ny,)),
            dma((quarters, ny)),
            dma((nc,)),
            dma((nc,)),
            dma((quarters, max(1, ny - 1), nc)),
            dma(()),
            dma(()),
            dma((parts,)),
            dma((parts,)),
            dma(()),
            dma(()),
        ],
        compiler_params=pltpu.CompilerParams(
            collective_id=0, has_side_effects=True, vmem_limit_bytes=56 * 1024 * 1024
        ),
        name="layer",
    )(
        residual_tiles[0],
        picture_label_tile,
        prenorm_multiplier[None],
        triple_projector,
        logit_scaling,
        final_projector,
        binarizer_projector.T,
        binarizer_offset[None],
    )
    mixed, codes, ent = pl.pallas_call(
        put_kernel,
        out_shape=(
            jax.ShapeDtypeStruct((rows, width), bf16),
            jax.ShapeDtypeStruct((bits, 1, rows), f32),
            jax.ShapeDtypeStruct((1, bits), f32),
        ),
        in_specs=[vmem] * 3,
        out_specs=[hbm] * 3,
        scratch_shapes=[dma((3,))],
        name="put",
    )(*(pltpu.with_memory_space_constraint(v, pltpu.VMEM) for v in (mixed, codes, ent)))
    return mixed[None], jnp.swapaxes(codes, 0, 1), ent[0]


def solution(mesh):
    ndp, n = mesh.shape["dp"], mesh.shape["seq"]
    nx = math.isqrt(ndp // 2)
    if nx < 1 or ndp % nx:
        nx = 1
    nc = 2 if n % 2 == 0 else 1
    cfg = {"nz": ndp // nx, "nx": nx, "ny": n // nc, "nc": nc}
    return jax.shard_map(
        functools.partial(on_device, cfg),
        mesh=mesh,
        in_specs=(
            P("dp", "seq", None),
            P("dp", "seq"),
            P(),
            P("dp", None),
            P(),
            P("dp", None),
            P(),
            P(),
        ),
        out_specs=(P("dp", "seq", None), P("dp", None, "seq"), P()),
        check_vma=False,
    )
```

```python
import functools
import math

import jax
import jax.numpy as jnp
from jax import lax
from jax.experimental import pallas as pl
from jax.experimental.pallas import tpu as pltpu
from jax.sharding import PartitionSpec as P

EPS = 1e-06
MESH = pl.DeviceIdType.MESH
LANES = 128
SAME = 640.0


def layer_kernel(
    cfg,
    x_ref,
    ids_ref,
    gain_hbm,
    w_ref,
    scale_hbm,
    wo_ref,
    bits_hbm,
    off_hbm,
    mixed_ref,
    codes_ref,
    ent_ref,
    wg,
    wog,
    xg,
    idg,
    normed,
    qs,
    ks,
    vs,
    ao,
    ag,
    stats,
    gain_ref,
    scale_ref,
    bits_ref,
    off_ref,
    local_sem,
    wz_s,
    wz_r,
    wx_s,
    wx_r,
    wt_s,
    wt_r,
    oz_s,
    oz_r,
    ox_s,
    ox_r,
    oy_s,
    oy_r,
    oc_s,
    oc_r,
    xy_s,
    xy_r,
    xc_s,
    own_r,
    xc_r,
    id_s,
    id_r,
    at_s,
    at_r,
    st_s,
    st_r,
):
    nz, nx, ny, nc = cfg["nz"], cfg["nx"], cfg["ny"], cfg["nc"]
    n = ny * nc
    ndp = nz * nx
    heads, channel = cfg["heads"], cfg["channel"]
    parts, quarters = cfg["parts"], cfg["quarters"]
    rows, width = x_ref.shape
    shard = w_ref.shape[0]
    cols = width // n
    pc = cols // parts
    sub = width // (nc * ny)
    seq_len = rows * n
    bits = bits_ref.shape[0]
    dp = lax.axis_index("dp")
    me = lax.axis_index("seq")
    z = dp // nx
    x = dp % nx
    y = me // nc
    core = me % nc

    def dp_at(zz, xx):
        return zz * nx + xx

    def seq_at(yy, cc):
        return yy * nc + cc

    def remote(src, dst, ss, rs, d, s):
        return pltpu.make_async_remote_copy(
            src_ref=src, dst_ref=dst, send_sem=ss, recv_sem=rs, device_id=(d, s), device_id_type=MESH
        )

    def arrive(slot, sem):
        remote(slot, slot, sem, sem, dp, me).wait_recv()

    def left(slot, sem):
        remote(slot, slot, sem, sem, dp, me).wait_send()

    def shard_rows(zz, xx):
        return pl.ds(pl.multiple_of(dp_at(zz, xx) * shard, shard), shard)

    def w_slot_of(h):
        return lambda zz, xx: wg.at[h, shard_rows(zz, xx), :]

    w_slots = [w_slot_of(h) for h in range(parts)]
    x_rows = rows // quarters

    def x_piece(member, q):
        return xg.at[member, pl.ds(q * x_rows, x_rows), :]

    def o_slot(zz, xx):
        return wog.at[core, :, shard_rows(zz, xx), :]

    def o_sub(yy, zz, xx):
        return wog.at[core, yy, shard_rows(zz, xx), :]

    lo = jnp.minimum(z, nz - 1 - z)

    def piece(i):
        near = z - (i + 1) // 2 if i % 2 else z + (i + 1) // 2
        far = jnp.where(z > nz - 1 - z, z - (i - lo), z + (i - lo))
        return jnp.where(i <= 2 * lo, near, far) if i else z

    def line_start(slot, ss, rs, i, when=True):
        if nz == 1:
            return
        p = piece(i)
        here = slot(p, x)
        to_left = remote(here, here, ss.at[0], rs.at[p], dp_at(jnp.maximum(z - 1, 0), x), me)
        to_right = remote(here, here, ss.at[1], rs.at[p], dp_at(jnp.minimum(z + 1, nz - 1), x), me)
        for wanted, hop in (
            (jnp.logical_and(p >= z, z > 0), to_left),
            (jnp.logical_and(p <= z, z < nz - 1), to_right),
        ):

            @pl.when(wanted if when is True else jnp.logical_and(wanted, when))
            def _(hop=hop):
                hop.start()

    def line_left(block, ss):
        for zz in range(nz if nz > 1 else 0):

            @pl.when(z == zz)
            def _(zz=zz):
                if zz > 0:
                    left(block(nz - zz), ss.at[0])
                if zz < nz - 1:
                    left(block(zz + 1), ss.at[1])

    def across(slot, ss, rs, i):
        p = piece(i)
        for k in range(1, nx):
            remote(slot(p, x), slot(p, x), ss, rs(k), dp_at(z, (x + k) % nx), me).start()

    def share(here):
        for k in range(1, nc):
            remote(here, here, oc_s.at[k], oc_r.at[k], dp, seq_at(y, (core + k) % nc)).start()

    def whole(i):
        return i >= nz - 2 or ny == 1

    def o_crossing(i, k, d):
        p, xx = piece(i), (x - k + nx) % nx
        return o_slot(p, xx) if whole(i) else o_sub((y - d + ny) % ny, p, xx)

    def o_line_start(i, when=True):
        line_start(o_slot, oz_s, oz_r, i, when)

    def o_cross(i):
        slot = o_slot if whole(i) else lambda zz, xx: o_sub(y, zz, xx)
        across(slot, ox_s.at[int(whole(i))], lambda k: ox_r.at[i, k], i)

    def o_line(i):
        p = piece(i)
        arrive(o_slot(p, x), oz_r.at[p])
        o_line_start(i)
        o_cross(i)
        share(o_slot(p, x))

    def o_crossed(i):
        for k in range(1, nx):
            here = o_crossing(i, k, 0)
            arrive(here, ox_r.at[i, k])
            if not whole(i):
                for d in range(1, ny):
                    remote(
                        here, here, oy_s.at[d], oy_r.at[i, k, d], dp, seq_at((y + d) % ny, core)
                    ).start()
            share(here)

    def o_last(i):
        for k in range(1, nx):
            for d in range(1, 1 if whole(i) else ny):
                arrive(o_crossing(i, k, d), oy_r.at[i, k, d])
                share(o_crossing(i, k, d))

    def o_shared():
        for k in range(1, nc):
            arrive(wog.at[(core - k + nc) % nc], oc_r.at[k])

    own_w, own_o = [], []
    for h in range(parts):
        for part in range(3):
            own_w.append(
                pltpu.make_async_copy(
                    w_ref.at[:, pl.ds(pl.multiple_of(part * width + me * cols + h * pc, LANES), pc)],
                    wg.at[h, shard_rows(z, x), pl.ds(part * pc, pc)],
                    local_sem.at[0],
                )
            )
    own_x = pltpu.make_async_copy(x_ref, xg.at[me], local_sem.at[1])
    own_id = pltpu.make_async_copy(ids_ref, idg.at[me], local_sem.at[2])
    for yy in range(ny):
        own_o.append(
            pltpu.make_async_copy(
                wo_ref.at[:, pl.ds(pl.multiple_of((core * ny + yy) * sub, LANES), sub)],
                o_sub(yy, z, x),
                local_sem.at[3],
            )
        )
    own_small = [
        pltpu.make_async_copy(src, dst, local_sem.at[4 + i])
        for i, (src, dst) in enumerate(
            ((gain_hbm, gain_ref), (scale_hbm, scale_ref), (bits_hbm, bits_ref), (off_hbm, off_ref))
        )
    ]
    for c in own_w + [own_id, own_x] + own_small + own_o:
        c.start()

    barrier = pltpu.get_barrier_semaphore()

    def greet(d, s):
        pl.semaphore_signal(barrier, inc=1, device_id=(d, s), device_id_type=MESH)

    for i in range(1, n):
        greet(dp, (me + i) % n)
    for k in range(1, nx):
        greet(dp_at(z, (x + k) % nx), me)

    @pl.when(z > 0)
    def _():
        greet(dp_at(z - 1, x), me)

    @pl.when(z < nz - 1)
    def _():
        greet(dp_at(z + 1, x), me)

    ends = jnp.where(z > 0, 1, 0) + jnp.where(z < nz - 1, 1, 0)
    pl.semaphore_wait(barrier, n - 1 + nx - 1 + ends)

    own_block = wg.at[:, shard_rows(z, x), :]
    pltpu.make_async_copy(own_block, own_block, local_sem.at[0]).wait()

    turning = nz > 1 and nx > 1
    last = parts - 1

    def w_forward(i, h):
        line_start(w_slots[h], wz_s, wz_r.at[h], i)
        arriving = wt_r.at[0] if turning and h == last and i == 0 else wx_r.at[h]
        if turning and h == last and i == 1:

            @pl.when(lo > 0)
            def _():
                across(w_slots[h], wx_s.at[h], lambda k: arriving, i)

        else:
            across(w_slots[h], wx_s.at[h], lambda k: arriving, i)

    def w_rows(h, count):
        return wg.at[h, pl.ds(0, count * (nx - 1) * shard), :]

    def w_turned():
        arrive(w_rows(last, 1), wt_r.at[0])
        for side, wanted, zz in ((0, z == 1, z - 1), (1, z == nz - 2, z + 1)):

            @pl.when(wanted)
            def _(side=side, zz=zz):
                for k in range(1, nx):
                    here = w_slots[last](z, (x - k + nx) % nx)
                    remote(here, here, wt_s.at[side], wt_r.at[1], dp_at(zz, x), me).start()

    for h in range(parts):
        w_forward(0, h)
    own_id.wait()
    for i in range(1, n):
        remote(idg.at[me], idg.at[me], id_s, id_r, dp, (me + i) % n).start()
    own_x.wait()
    for q in range(quarters):
        for i in range(1, ny):
            mine = x_piece(me, q)
            remote(mine, mine, xy_s.at[i], xy_r.at[q, i], dp, seq_at((y + i) % ny, core)).start()
    for k in range(1, nc):
        remote(xg.at[me], xg.at[me], xc_s.at[k], own_r.at[k], dp, seq_at(y, (core + k) % nc)).start()

    for c in own_small:
        c.wait()
    own_block = o_slot(z, x)
    pltpu.make_async_copy(own_block, own_block, local_sem.at[3]).wait()
    o_line_start(0, lo == 0)

    gain = gain_ref[...]
    block = math.gcd(x_rows, 64)

    def norm_rows(member, q, count=1):
        start = pl.multiple_of(member * rows, rows)

        def body(b, _):
            r0 = pl.multiple_of(q * x_rows + b * block, block)
            wide = xg[member, pl.ds(r0, block), :].astype(jnp.float32)
            ms = jnp.mean(wide * wide, axis=-1, keepdims=True)
            out = (wide * lax.rsqrt(ms + EPS) * gain).astype(jnp.bfloat16)
            normed[pl.ds(start + r0, block), :] = out
            return 0

        lax.fori_loop(0, count * x_rows // block, body, 0)

    norm_rows(me, 0, quarters)
    arrive(idg.at[pl.ds(0, n - 1)], id_r)
    lane_ids = lax.broadcasted_iota(jnp.int32, (rows, LANES), 1).astype(jnp.float32)
    for m in range(n):
        column = jnp.transpose(jnp.broadcast_to(idg[m].astype(jnp.float32), (LANES, rows)))
        hot = jnp.where(column == lane_ids, 1.0, 0.0)
        r = pl.ds(m * rows, rows)
        for h in range(parts):
            qs[h, r, pc:] = (hot * SAME).astype(jnp.bfloat16)
            ks[h, r, pc:] = hot.astype(jnp.bfloat16)
            vs[h, r, pc:] = jnp.ones((rows, pc), jnp.bfloat16)
    for k in range(1, nc):
        other = seq_at(y, (core - k + nc) % nc)
        arrive(xg.at[other], own_r.at[k])
        norm_rows(other, 0, quarters)

    def x_arrived(i, q):
        source = seq_at((y - i + ny) % ny, core)
        slot = x_piece(source, q)
        arrive(slot, xy_r.at[q, i])
        for k in range(1, nc):
            remote(slot, slot, xc_s.at[k], xc_r.at[q, i - 1, k], dp, seq_at(y, (core + k) % nc)).start()
        norm_rows(source, q)

    def x_shared(i, q):
        for k in range(1, nc):
            other = seq_at((y - i + ny) % ny, (core - k + nc) % nc)
            arrive(x_piece(other, q), xc_r.at[q, i - 1, k])
            norm_rows(other, q)

    def w_arrived(i, h):
        arrive(w_slots[h](piece(i), x), wz_r.at[h, piece(i)])
        w_forward(i, h)

    events = []
    for i in range(1, nz):
        for h in range(parts):
            events.append((((i - 1) * parts + h + 1) * shard * 3 * pc, 0, i, h))
    for i in range(1, ny):
        for q in range(quarters):
            events.append((((i - 1) * quarters + q + 1) * x_rows * width, 1, i, q))
    waiting = []
    if turning:
        events.append((parts * shard * 3 * pc + 1, 2, 0, 0))
    for _, stream, i, j in sorted(events):
        if stream == 0:
            w_arrived(i, j)
        elif stream == 2:
            w_turned()
        else:
            x_arrived(i, j)
            waiting.append((i, j))
            if len(waiting) > 1:
                x_shared(*waiting.pop(0))
    o_line_start(0, lo > 0)
    o_cross(0)
    share(o_slot(z, x))
    for late in waiting:
        x_shared(*late)

    row_block = 256
    blocks = seq_len // row_block

    def group_of(shape, dim):
        return lax.div(lax.broadcasted_iota(jnp.int32, shape, dim), jnp.int32(channel))

    pair = (2 * pc, 2 * pc)
    same_head = jnp.where(group_of(pair, 0) == group_of(pair, 1), 1.0, 0.0).astype(jnp.bfloat16)
    part_heads = pc // channel

    def project(h):
        scale_row = jnp.ones((1, 2 * pc), jnp.float32)
        for g in range(part_heads):
            value = scale_ref[me * heads + h * part_heads + g] / math.sqrt(channel)
            scale_row = jnp.where(group_of((1, 2 * pc), 1) == g, value, scale_row)
        if turning and h == last:

            @pl.when(lo == 0)
            def _():
                arrive(w_rows(h, 1), wt_r.at[1])
                if nz > 2:
                    arrive(w_rows(h, nz - 2), wx_r.at[h])

            @pl.when(lo > 0)
            def _():
                arrive(w_rows(h, nz - 1), wx_r.at[h])

        elif nx > 1:
            arrive(w_rows(h, nz), wx_r.at[h])

        for b in range(blocks):
            r = pl.ds(b * row_block, row_block)
            joined = jnp.dot(normed[r, :], wg[h], preferred_element_type=jnp.float32).astype(jnp.bfloat16)
            qk = joined[:, : 2 * pc].astype(jnp.float32)
            square = qk * qk
            high = square.astype(jnp.bfloat16)
            low = (square - high.astype(jnp.float32)).astype(jnp.bfloat16)
            total = jnp.dot(high, same_head, preferred_element_type=jnp.float32) + jnp.dot(
                low, same_head, preferred_element_type=jnp.float32
            )
            qk = (qk * lax.rsqrt(total / channel + EPS) * scale_row).astype(jnp.bfloat16)
            qs[h, r, :pc] = qk[:, :pc]
            ks[h, r, :pc] = qk[:, pc:]
            vs[h, r, :pc] = joined[:, 2 * pc :]

    q_block = cfg["q_block"]
    lane_head = group_of((q_block, pc), 1)

    def stage_target(t, sign):
        dy = (t // nc + 1) % ny
        dc = (t + 1) % nc
        if sign > 0:
            return seq_at((y + dy) % ny, (core + dc) % nc)
        return seq_at((y - dy + ny) % ny, (core - dc + nc) % nc)

    def a2a(h, t):
        j = stage_target(t, 1)
        return remote(ao.at[h, j], ag.at[h, me], at_s.at[h], at_r.at[h], dp, j)

    def attend(h, stages):
        for t in stages:
            j = stage_target(t, 1)
            for part in range(rows // q_block):
                r = pl.ds(pl.multiple_of(j * rows + part * q_block, q_block), q_block)
                qb = qs[h, r, :]
                out = jnp.zeros((q_block, pc), jnp.float32)
                for g in range(part_heads):
                    mine = lane_head == g
                    qh = jnp.concatenate([jnp.where(mine, qb[:, :pc], jnp.zeros_like(qb[:, :pc])), qb[:, pc:]], axis=1)
                    s = lax.dot_general(qh, ks[h], (((1,), (1,)), ((), ())), preferred_element_type=jnp.float32)
                    p = jnp.exp(s - jnp.max(s, axis=-1, keepdims=True))
                    o = jnp.dot(p.astype(jnp.bfloat16), vs[h], preferred_element_type=jnp.float32)
                    out = jnp.where(mine, o[:, :pc] / o[:, pc:], out)
                ao[h, j, pl.ds(part * q_block, q_block), :] = out.astype(jnp.bfloat16)
        for t in stages:
            if t < n - 1:
                a2a(h, t).start()

    chores = [functools.partial(o_line, i) for i in range(1, nz - 1)]
    for c in chores:
        c()
    half = n // 2
    for h in range(parts):
        project(h)
        if h == 0:
            o_crossed(0)
        attend(h, range(half))
        if h == 0 and nz > 1:
            o_crossed(1)
        attend(h, range(half, n))
        if h == 0 and nz > 1:
            o_line(nz - 1)
    for i in range(2, nz):
        o_crossed(i)
        o_last(i - 2)
    for i in range(max(0, nz - 2), nz):
        o_last(i)
    o_shared()

    for h in range(parts):
        arrive(ag.at[h, pl.ds(0, n - 1)], at_r.at[h])
        ag[h, me] = ao[h, me]

    attention = jnp.concatenate([ag[h, m] for m in range(n) for h in range(parts)], axis=1)
    for g in range(nc * ny):
        lanes = slice(g * sub, (g + 1) * sub)
        prod = jnp.dot(attention, wog[g // ny, g % ny], preferred_element_type=jnp.float32)
        mixed_ref[:, lanes] = (xg[me, :, lanes].astype(jnp.float32) + prod).astype(jnp.bfloat16)

    logits = lax.dot_general(
        bits_ref[...], mixed_ref[...], (((1,), (1,)), ((), ())), preferred_element_type=jnp.float32
    )
    eye = lax.broadcasted_iota(jnp.int32, (bits, bits), 0) == lax.broadcasted_iota(
        jnp.int32, (bits, bits), 1
    )
    offset = jnp.sum(jnp.where(eye, off_ref[...], 0.0), axis=1, keepdims=True)
    probs = jax.nn.sigmoid(4.0 * (logits + offset))
    lanes_eye = lax.broadcasted_iota(jnp.int32, (bits, LANES), 0) == lax.broadcasted_iota(
        jnp.int32, (bits, LANES), 1
    )
    own_sums = jnp.sum(probs, axis=1, keepdims=True)
    count = n * ndp
    mine = dp * n + me
    stats[mine, :, :] = jnp.sum(jnp.where(lanes_eye, own_sums, 0.0), axis=0, keepdims=True)

    def tell(i, _):
        zz = jnp.where(2 * z < nz, nz - 1 - i, i)
        for k in range(nx):
            for m in range(n):
                there = remote(
                    stats.at[mine], stats.at[mine], st_s, st_r, dp_at(zz, (x + k) % nx), (me + m) % n
                )
                if k or m:
                    there.start()
                else:
                    pl.when(zz != z)(there.start)
        return 0

    lax.fori_loop(0, nz, tell, 0)
    others = stats.at[pl.ds(0, count - 1)]
    arrive(others, st_r)
    total = jnp.sum(stats[...], axis=0)
    marginal = total / (seq_len * ndp)
    line = marginal[:, :bits]
    ent_ref[...] = -(line * jnp.log(line) + (1.0 - line) * jnp.log(1.0 - line))
    codes = probs - jnp.sum(jnp.where(lanes_eye, marginal, 0.0), axis=1, keepdims=True)
    for b in range(bits):
        codes_ref[b] = codes[b : b + 1, :]

    left(others, st_s)
    line_left(lambda m: wg.at[:, pl.ds(0, m * shard), :], wz_s)
    line_left(lambda m: wog.at[0, :, pl.ds(0, m * shard), :], oz_s)
    halves = [i for i in range(nz) if not whole(i)]
    if nx > 1:
        for h in range(parts - 1 if turning else parts):
            left(w_rows(h, nz), wx_s.at[h])
        if turning:
            for wanted, ref, sem in (
                (lo == 0, w_rows(last, nz - 1), wx_s.at[last]),
                (lo > 0, w_rows(last, nz), wx_s.at[last]),
                (z == 1, w_rows(last, 1), wt_s.at[0]),
                (z == nz - 2, w_rows(last, 1), wt_s.at[1]),
            ):

                @pl.when(wanted)
                def _(ref=ref, sem=sem):
                    left(ref, sem)

        if halves:
            block = wog.at[0, 0, pl.ds(0, len(halves) * (nx - 1) * shard), :]
            left(block, ox_s.at[0])
            for d in range(1, ny):
                left(block, oy_s.at[d])
        if len(halves) < nz:
            left(wog.at[0, :, pl.ds(0, (nz - len(halves)) * (nx - 1) * shard), :], ox_s.at[1])
    for k in range(1, nc):
        left(wog.at[core], oc_s.at[k])
        left(xg.at[pl.ds(0, ny)], xc_s.at[k])
    for i in range(1, ny):
        left(xg.at[me], xy_s.at[i])
    left(idg.at[pl.ds(0, n - 1)], id_s)
    for h in range(parts):
        left(ag.at[h, pl.ds(0, n - 1)], at_s.at[h])


def put_kernel(mixed_ref, codes_ref, ent_ref, mixed_out, codes_out, ent_out, sems):
    pairs = ((mixed_ref, mixed_out), (codes_ref, codes_out), (ent_ref, ent_out))
    copies = [pltpu.make_async_copy(src, dst, sems.at[i]) for i, (src, dst) in enumerate(pairs)]
    for c in copies:
        c.start()
    for c in copies:
        c.wait()


def on_device(
    cfg,
    residual_tiles,
    picture_label_tile,
    prenorm_multiplier,
    triple_projector,
    logit_scaling,
    final_projector,
    binarizer_projector,
    binarizer_offset,
):
    nz, nx, ny, nc = cfg["nz"], cfg["nx"], cfg["ny"], cfg["nc"]
    n, ndp = ny * nc, nz * nx
    _, rows, width = residual_tiles.shape
    heads_all = logit_scaling.shape[0]
    bits = binarizer_projector.shape[1]
    cols = width // n
    shard = triple_projector.shape[0]
    seq_len = rows * n
    parts = cols // LANES if cols % LANES == 0 else 1
    pc, sub = cols // parts, width // (nc * ny)
    quarters = 4 if rows % 128 == 0 else 1
    cfg = dict(
        cfg,
        heads=heads_all // n,
        channel=width // heads_all,
        q_block=min(256, rows),
        parts=parts,
        quarters=quarters,
    )
    dma = pltpu.SemaphoreType.DMA
    vmem, hbm = pl.BlockSpec(memory_space=pltpu.VMEM), pl.BlockSpec(memory_space=pl.ANY)
    bf16, f32 = jnp.bfloat16, jnp.float32
    mixed, codes, ent = pl.pallas_call(
        functools.partial(layer_kernel, cfg),
        out_shape=(
            pltpu.VMEM((rows, width), bf16),
            pltpu.VMEM((bits, 1, rows), f32),
            pltpu.VMEM((1, bits), f32),
        ),
        in_specs=[hbm] * 8,
        out_specs=(vmem, vmem, vmem),
        scratch_shapes=[
            pltpu.VMEM((parts, width, 3 * pc), bf16),
            pltpu.VMEM((nc, ny, width, sub), bf16),
            pltpu.VMEM((n, rows, width), bf16),
            pltpu.VMEM((n, 1, rows), jnp.int32),
            pltpu.VMEM((seq_len, width), bf16),
            pltpu.VMEM((parts, seq_len, pc + LANES), bf16),
            pltpu.VMEM((parts, seq_len, pc + LANES), bf16),
            pltpu.VMEM((parts, seq_len, 2 * pc), bf16),
            pltpu.VMEM((parts, n, rows, pc), bf16),
            pltpu.VMEM((parts, n, rows, pc), bf16),
            pltpu.VMEM((n * ndp, 1, LANES), f32),
            pltpu.VMEM((1, width), f32),
            pltpu.SMEM((heads_all,), f32),
            pltpu.VMEM((bits, width), bf16),
            pltpu.VMEM((1, bits), f32),
            dma((8,)),
            dma((2,)),
            dma((parts, nz)),
            dma((parts,)),
            dma((parts,)),
            dma((2,)),
            dma((2,)),
            dma((2,)),
            dma((nz,)),
            dma((2,)),
            dma((nz, nx)),
            dma((ny,)),
            dma((max(1, nz - 2), nx, ny)),
            dma((nc,)),
            dma((nc,)),
            dma((ny,)),
            dma((quarters, ny)),
            dma((nc,)),
            dma((nc,)),
            dma((quarters, max(1, ny - 1), nc)),
            dma(()),
            dma(()),
            dma((parts,)),
            dma((parts,)),
            dma(()),
            dma(()),
        ],
        compiler_params=pltpu.CompilerParams(
            collective_id=0, has_side_effects=True, vmem_limit_bytes=56 * 1024 * 1024
        ),
        name="layer",
    )(
        residual_tiles[0],
        picture_label_tile,
        prenorm_multiplier[None],
        triple_projector,
        logit_scaling,
        final_projector,
        binarizer_projector.T,
        binarizer_offset[None],
    )
    mixed, codes, ent = pl.pallas_call(
        put_kernel,
        out_shape=(
            jax.ShapeDtypeStruct((rows, width), bf16),
            jax.ShapeDtypeStruct((bits, 1, rows), f32),
            jax.ShapeDtypeStruct((1, bits), f32),
        ),
        in_specs=[vmem] * 3,
        out_specs=[hbm] * 3,
        scratch_shapes=[dma((3,))],
        name="put",
    )(*(pltpu.with_memory_space_constraint(v, pltpu.VMEM) for v in (mixed, codes, ent)))
    return mixed[None], jnp.swapaxes(codes, 0, 1), ent[0]


def solution(mesh):
    ndp, n = mesh.shape["dp"], mesh.shape["seq"]
    nx = math.isqrt(ndp // 2)
    if nx < 1 or ndp % nx:
        nx = 1
    nc = 2 if n % 2 == 0 else 1
    cfg = {"nz": ndp // nx, "nx": nx, "ny": n // nc, "nc": nc}
    return jax.shard_map(
        functools.partial(on_device, cfg),
        mesh=mesh,
        in_specs=(
            P("dp", "seq", None),
            P("dp", "seq"),
            P(),
            P("dp", None),
            P(),
            P("dp", None),
            P(),
            P(),
        ),
        out_specs=(P("dp", "seq", None), P("dp", None, "seq"), P()),
        check_vma=False,
    )
```

```python
import functools
import math

import jax
import jax.numpy as jnp
from jax import lax
from jax.experimental import pallas as pl
from jax.experimental.pallas import tpu as pltpu
from jax.sharding import PartitionSpec as P

EPS = 1e-06
MESH = pl.DeviceIdType.MESH
LANES = 128
SAME = 640.0


def layer_kernel(
    cfg,
    x_ref,
    ids_ref,
    gain_hbm,
    w_ref,
    scale_hbm,
    wo_ref,
    bits_hbm,
    off_hbm,
    mixed_ref,
    codes_ref,
    ent_ref,
    wg,
    wog,
    xg,
    idg,
    normed,
    qs,
    ks,
    vs,
    ao,
    ag,
    stats,
    gain_ref,
    scale_ref,
    bits_ref,
    off_ref,
    local_sem,
    wz_s,
    wz_r,
    wx_s,
    wx_r,
    oz_s,
    oz_r,
    ox_s,
    ox_r,
    oy_s,
    oy_r,
    oc_s,
    oc_r,
    xy_s,
    xy_r,
    xc_s,
    own_r,
    xc_r,
    id_s,
    id_r,
    at_s,
    at_r,
    st_s,
    st_r,
):
    nz, nx, ny, nc = cfg["nz"], cfg["nx"], cfg["ny"], cfg["nc"]
    n = ny * nc
    ndp = nz * nx
    heads, channel = cfg["heads"], cfg["channel"]
    parts, quarters = cfg["parts"], cfg["quarters"]
    rows, width = x_ref.shape
    shard = w_ref.shape[0]
    cols = width // n
    pc = cols // parts
    sub = width // (nc * ny)
    seq_len = rows * n
    bits = bits_ref.shape[0]
    dp = lax.axis_index("dp")
    me = lax.axis_index("seq")
    z = dp // nx
    x = dp % nx
    y = me // nc
    core = me % nc

    def dp_at(zz, xx):
        return zz * nx + xx

    def seq_at(yy, cc):
        return yy * nc + cc

    def remote(src, dst, ss, rs, d, s):
        return pltpu.make_async_remote_copy(
            src_ref=src, dst_ref=dst, send_sem=ss, recv_sem=rs, device_id=(d, s), device_id_type=MESH
        )

    def arrive(slot, sem):
        remote(slot, slot, sem, sem, dp, me).wait_recv()

    def left(slot, sem):
        remote(slot, slot, sem, sem, dp, me).wait_send()

    def shard_rows(zz, xx):
        return pl.ds(pl.multiple_of(dp_at(zz, xx) * shard, shard), shard)

    def w_slot_of(h):
        return lambda zz, xx: wg.at[h, shard_rows(zz, xx), :]

    w_slots = [w_slot_of(h) for h in range(parts)]
    x_rows = rows // quarters

    def x_piece(member, q):
        return xg.at[member, pl.ds(q * x_rows, x_rows), :]

    def o_slot(zz, xx):
        return wog.at[core, :, shard_rows(zz, xx), :]

    def o_sub(yy, zz, xx):
        return wog.at[core, yy, shard_rows(zz, xx), :]

    lo = jnp.minimum(z, nz - 1 - z)

    def piece(i):
        near = z - (i + 1) // 2 if i % 2 else z + (i + 1) // 2
        far = jnp.where(z > nz - 1 - z, z - (i - lo), z + (i - lo))
        return jnp.where(i <= 2 * lo, near, far) if i else z

    def line_start(slot, ss, rs, i, when=True):
        if nz == 1:
            return
        p = piece(i)
        here = slot(p, x)
        to_left = remote(here, here, ss.at[0], rs.at[p], dp_at(jnp.maximum(z - 1, 0), x), me)
        to_right = remote(here, here, ss.at[1], rs.at[p], dp_at(jnp.minimum(z + 1, nz - 1), x), me)
        for wanted, hop in (
            (jnp.logical_and(p >= z, z > 0), to_left),
            (jnp.logical_and(p <= z, z < nz - 1), to_right),
        ):

            @pl.when(wanted if when is True else jnp.logical_and(wanted, when))
            def _(hop=hop):
                hop.start()

    def line_left(block, ss):
        for zz in range(nz if nz > 1 else 0):

            @pl.when(z == zz)
            def _(zz=zz):
                if zz > 0:
                    left(block(nz - zz), ss.at[0])
                if zz < nz - 1:
                    left(block(zz + 1), ss.at[1])

    def across(slot, ss, rs, i):
        p = piece(i)
        for k in range(1, nx):
            remote(slot(p, x), slot(p, x), ss, rs(k), dp_at(z, (x + k) % nx), me).start()

    def share(here):
        for k in range(1, nc):
            remote(here, here, oc_s.at[k], oc_r.at[k], dp, seq_at(y, (core + k) % nc)).start()

    def whole(i):
        return i >= nz - 2 or ny == 1

    def o_crossing(i, k, d):
        p, xx = piece(i), (x - k + nx) % nx
        return o_slot(p, xx) if whole(i) else o_sub((y - d + ny) % ny, p, xx)

    def o_line_start(i, when=True):
        line_start(o_slot, oz_s, oz_r, i, when)

    def o_cross(i):
        slot = o_slot if whole(i) else lambda zz, xx: o_sub(y, zz, xx)
        across(slot, ox_s.at[int(whole(i))], lambda k: ox_r.at[i, k], i)

    def o_line(i):
        p = piece(i)
        arrive(o_slot(p, x), oz_r.at[p])
        o_line_start(i)
        o_cross(i)
        share(o_slot(p, x))

    def o_crossed(i):
        for k in range(1, nx):
            here = o_crossing(i, k, 0)
            arrive(here, ox_r.at[i, k])
            if not whole(i):
                for d in range(1, ny):
                    remote(
                        here, here, oy_s.at[d], oy_r.at[i, k, d], dp, seq_at((y + d) % ny, core)
                    ).start()
            share(here)

    def o_last(i):
        for k in range(1, nx):
            for d in range(1, 1 if whole(i) else ny):
                arrive(o_crossing(i, k, d), oy_r.at[i, k, d])
                share(o_crossing(i, k, d))

    def o_shared():
        for k in range(1, nc):
            arrive(wog.at[(core - k + nc) % nc], oc_r.at[k])

    own_w, own_o = [], []
    for h in range(parts):
        for part in range(3):
            own_w.append(
                pltpu.make_async_copy(
                    w_ref.at[:, pl.ds(pl.multiple_of(part * width + me * cols + h * pc, LANES), pc)],
                    wg.at[h, shard_rows(z, x), pl.ds(part * pc, pc)],
                    local_sem.at[0],
                )
            )
    own_x = pltpu.make_async_copy(x_ref, xg.at[me], local_sem.at[1])
    own_id = pltpu.make_async_copy(ids_ref, idg.at[me], local_sem.at[2])
    for yy in range(ny):
        own_o.append(
            pltpu.make_async_copy(
                wo_ref.at[:, pl.ds(pl.multiple_of((core * ny + yy) * sub, LANES), sub)],
                o_sub(yy, z, x),
                local_sem.at[3],
            )
        )
    own_small = [
        pltpu.make_async_copy(src, dst, local_sem.at[4 + i])
        for i, (src, dst) in enumerate(
            ((gain_hbm, gain_ref), (scale_hbm, scale_ref), (bits_hbm, bits_ref), (off_hbm, off_ref))
        )
    ]
    for c in own_w + [own_id, own_x] + own_small + own_o:
        c.start()

    barrier = pltpu.get_barrier_semaphore()

    def greet(d, s):
        pl.semaphore_signal(barrier, inc=1, device_id=(d, s), device_id_type=MESH)

    for i in range(1, n):
        greet(dp, (me + i) % n)
    for k in range(1, nx):
        greet(dp_at(z, (x + k) % nx), me)

    @pl.when(z > 0)
    def _():
        greet(dp_at(z - 1, x), me)

    @pl.when(z < nz - 1)
    def _():
        greet(dp_at(z + 1, x), me)

    ends = jnp.where(z > 0, 1, 0) + jnp.where(z < nz - 1, 1, 0)
    pl.semaphore_wait(barrier, n - 1 + nx - 1 + ends)

    own_block = wg.at[:, shard_rows(z, x), :]
    pltpu.make_async_copy(own_block, own_block, local_sem.at[0]).wait()

    def w_along(i, h, when=True):
        line_start(w_slots[h], wz_s, wz_r.at[h], i, when)

    def w_across(i, h):
        across(w_slots[h], wx_s.at[h], lambda k: wx_r.at[h], i)

    for h in range(parts):
        w_along(0, h, True if h == 0 else lo == 0)
        w_across(0, h)
    own_id.wait()
    for i in range(1, n):
        remote(idg.at[me], idg.at[me], id_s, id_r, dp, (me + i) % n).start()
    own_x.wait()
    for q in range(quarters):
        for i in range(1, ny):
            mine = x_piece(me, q)
            remote(mine, mine, xy_s.at[i], xy_r.at[q, i], dp, seq_at((y + i) % ny, core)).start()
    for k in range(1, nc):
        remote(xg.at[me], xg.at[me], xc_s.at[k], own_r.at[k], dp, seq_at(y, (core + k) % nc)).start()

    for c in own_small:
        c.wait()
    own_block = o_slot(z, x)
    pltpu.make_async_copy(own_block, own_block, local_sem.at[3]).wait()
    o_line_start(0, lo == 0)

    gain = gain_ref[...]
    block = math.gcd(x_rows, 64)

    def norm_rows(member, q, count=1):
        start = pl.multiple_of(member * rows, rows)

        def body(b, _):
            r0 = pl.multiple_of(q * x_rows + b * block, block)
            wide = xg[member, pl.ds(r0, block), :].astype(jnp.float32)
            ms = jnp.mean(wide * wide, axis=-1, keepdims=True)
            out = (wide * lax.rsqrt(ms + EPS) * gain).astype(jnp.bfloat16)
            normed[pl.ds(start + r0, block), :] = out
            return 0

        lax.fori_loop(0, count * x_rows // block, body, 0)

    norm_rows(me, 0, quarters)
    arrive(idg.at[pl.ds(0, n - 1)], id_r)
    lane_ids = lax.broadcasted_iota(jnp.int32, (rows, LANES), 1).astype(jnp.float32)
    for m in range(n):
        column = jnp.transpose(jnp.broadcast_to(idg[m].astype(jnp.float32), (LANES, rows)))
        hot = jnp.where(column == lane_ids, 1.0, 0.0)
        r = pl.ds(m * rows, rows)
        for h in range(parts):
            qs[h, r, pc:] = (hot * SAME).astype(jnp.bfloat16)
            ks[h, r, pc:] = hot.astype(jnp.bfloat16)
            vs[h, r, pc:] = jnp.ones((rows, pc), jnp.bfloat16)
    for k in range(1, nc):
        other = seq_at(y, (core - k + nc) % nc)
        arrive(xg.at[other], own_r.at[k])
        norm_rows(other, 0, quarters)

    def x_arrived(i, q):
        source = seq_at((y - i + ny) % ny, core)
        slot = x_piece(source, q)
        arrive(slot, xy_r.at[q, i])
        for k in range(1, nc):
            remote(slot, slot, xc_s.at[k], xc_r.at[q, i - 1, k], dp, seq_at(y, (core + k) % nc)).start()
        norm_rows(source, q)

    def x_shared(i, q):
        for k in range(1, nc):
            other = seq_at((y - i + ny) % ny, (core - k + nc) % nc)
            arrive(x_piece(other, q), xc_r.at[q, i - 1, k])
            norm_rows(other, q)

    def w_arrived(i, h):
        arrive(w_slots[h](piece(i), x), wz_r.at[h, piece(i)])
        w_along(i, h)
        w_across(i, h)
        if (i, h) == (min(2, nz - 1), 0):
            for later in range(1, parts):
                w_along(0, later, lo > 0)

    events = []
    for i in range(1, nz):
        for h in range(parts):
            events.append(((h * (nz - 1) + i) * shard * 3 * pc, 0, i, h))
    for i in range(1, ny):
        for q in range(quarters):
            events.append((((i - 1) * quarters + q + 1) * x_rows * width, 1, i, q))
    waiting = []
    for _, stream, i, j in sorted(events):
        if stream == 0:
            w_arrived(i, j)
        else:
            x_arrived(i, j)
            waiting.append((i, j))
            if len(waiting) > 1:
                x_shared(*waiting.pop(0))
    o_line_start(0, lo > 0)
    o_cross(0)
    share(o_slot(z, x))
    for late in waiting:
        x_shared(*late)

    row_block = 256
    blocks = seq_len // row_block

    def group_of(shape, dim):
        return lax.div(lax.broadcasted_iota(jnp.int32, shape, dim), jnp.int32(channel))

    pair = (2 * pc, 2 * pc)
    same_head = jnp.where(group_of(pair, 0) == group_of(pair, 1), 1.0, 0.0).astype(jnp.bfloat16)
    part_heads = pc // channel
    last = parts - 1

    def project(h):
        scale_row = jnp.ones((1, 2 * pc), jnp.float32)
        for g in range(part_heads):
            value = scale_ref[me * heads + h * part_heads + g] / math.sqrt(channel)
            scale_row = jnp.where(group_of((1, 2 * pc), 1) == g, value, scale_row)
        if nx > 1:
            arrive(wg.at[h, pl.ds(0, nz * (nx - 1) * shard), :], wx_r.at[h])

        for b in range(blocks):
            r = pl.ds(b * row_block, row_block)
            joined = jnp.dot(normed[r, :], wg[h], preferred_element_type=jnp.float32).astype(jnp.bfloat16)
            qk = joined[:, : 2 * pc].astype(jnp.float32)
            square = qk * qk
            high = square.astype(jnp.bfloat16)
            low = (square - high.astype(jnp.float32)).astype(jnp.bfloat16)
            total = jnp.dot(high, same_head, preferred_element_type=jnp.float32) + jnp.dot(
                low, same_head, preferred_element_type=jnp.float32
            )
            qk = (qk * lax.rsqrt(total / channel + EPS) * scale_row).astype(jnp.bfloat16)
            qs[h, r, :pc] = qk[:, :pc]
            ks[h, r, :pc] = qk[:, pc:]
            vs[h, r, :pc] = joined[:, 2 * pc :]

    q_block = cfg["q_block"]
    lane_head = group_of((q_block, pc), 1)

    def stage_target(t, sign):
        dy = (t // nc + 1) % ny
        dc = (t + 1) % nc
        if sign > 0:
            return seq_at((y + dy) % ny, (core + dc) % nc)
        return seq_at((y - dy + ny) % ny, (core - dc + nc) % nc)

    def a2a(h, t):
        j = stage_target(t, 1)
        return remote(ao.at[h, j], ag.at[h, me], at_s.at[h], at_r.at[h], dp, j)

    def attend(h, stages):
        for t in stages:
            j = stage_target(t, 1)
            for part in range(rows // q_block):
                r = pl.ds(pl.multiple_of(j * rows + part * q_block, q_block), q_block)
                qb = qs[h, r, :]
                out = jnp.zeros((q_block, pc), jnp.float32)
                for g in range(part_heads):
                    mine = lane_head == g
                    qh = jnp.concatenate([jnp.where(mine, qb[:, :pc], jnp.zeros_like(qb[:, :pc])), qb[:, pc:]], axis=1)
                    s = lax.dot_general(qh, ks[h], (((1,), (1,)), ((), ())), preferred_element_type=jnp.float32)
                    p = jnp.exp(s - jnp.max(s, axis=-1, keepdims=True))
                    o = jnp.dot(p.astype(jnp.bfloat16), vs[h], preferred_element_type=jnp.float32)
                    out = jnp.where(mine, o[:, :pc] / o[:, pc:], out)
                ao[h, j, pl.ds(part * q_block, q_block), :] = out.astype(jnp.bfloat16)
        for t in stages:
            if t < n - 1:
                a2a(h, t).start()

    half = n // 2
    for h in range(last):
        project(h)
        attend(h, range(n))
    for i in range(1, nz - 1):
        o_line(i)
    o_crossed(0)
    project(last)
    attend(last, range(half))
    if nz > 1:
        o_crossed(1)
        o_line(nz - 1)
    attend(last, range(half, n))
    for i in range(2, nz):
        o_crossed(i)
        o_last(i - 2)
    for i in range(max(0, nz - 2), nz):
        o_last(i)
    o_shared()

    for h in range(parts):
        arrive(ag.at[h, pl.ds(0, n - 1)], at_r.at[h])
        ag[h, me] = ao[h, me]

    attention = jnp.concatenate([ag[h, m] for m in range(n) for h in range(parts)], axis=1)
    for g in range(nc * ny):
        lanes = slice(g * sub, (g + 1) * sub)
        prod = jnp.dot(attention, wog[g // ny, g % ny], preferred_element_type=jnp.float32)
        mixed_ref[:, lanes] = (xg[me, :, lanes].astype(jnp.float32) + prod).astype(jnp.bfloat16)

    logits = lax.dot_general(
        bits_ref[...], mixed_ref[...], (((1,), (1,)), ((), ())), preferred_element_type=jnp.float32
    )
    eye = lax.broadcasted_iota(jnp.int32, (bits, bits), 0) == lax.broadcasted_iota(
        jnp.int32, (bits, bits), 1
    )
    offset = jnp.sum(jnp.where(eye, off_ref[...], 0.0), axis=1, keepdims=True)
    probs = jax.nn.sigmoid(4.0 * (logits + offset))
    lanes_eye = lax.broadcasted_iota(jnp.int32, (bits, LANES), 0) == lax.broadcasted_iota(
        jnp.int32, (bits, LANES), 1
    )
    own_sums = jnp.sum(probs, axis=1, keepdims=True)
    count = n * ndp
    mine = dp * n + me
    stats[mine, :, :] = jnp.sum(jnp.where(lanes_eye, own_sums, 0.0), axis=0, keepdims=True)

    def tell(i, _):
        zz = jnp.where(2 * z < nz, nz - 1 - i, i)
        for k in range(nx):
            for m in range(n):
                there = remote(
                    stats.at[mine], stats.at[mine], st_s, st_r, dp_at(zz, (x + k) % nx), (me + m) % n
                )
                if k or m:
                    there.start()
                else:
                    pl.when(zz != z)(there.start)
        return 0

    lax.fori_loop(0, nz, tell, 0)
    others = stats.at[pl.ds(0, count - 1)]
    arrive(others, st_r)
    total = jnp.sum(stats[...], axis=0)
    marginal = total / (seq_len * ndp)
    line = marginal[:, :bits]
    ent_ref[...] = -(line * jnp.log(line) + (1.0 - line) * jnp.log(1.0 - line))
    codes = probs - jnp.sum(jnp.where(lanes_eye, marginal, 0.0), axis=1, keepdims=True)
    for b in range(bits):
        codes_ref[b] = codes[b : b + 1, :]

    left(others, st_s)
    line_left(lambda m: wg.at[:, pl.ds(0, m * shard), :], wz_s)
    line_left(lambda m: wog.at[0, :, pl.ds(0, m * shard), :], oz_s)
    halves = [i for i in range(nz) if not whole(i)]
    if nx > 1:
        for h in range(parts):
            left(wg.at[h, pl.ds(0, nz * (nx - 1) * shard), :], wx_s.at[h])
        if halves:
            block = wog.at[0, 0, pl.ds(0, len(halves) * (nx - 1) * shard), :]
            left(block, ox_s.at[0])
            for d in range(1, ny):
                left(block, oy_s.at[d])
        if len(halves) < nz:
            left(wog.at[0, :, pl.ds(0, (nz - len(halves)) * (nx - 1) * shard), :], ox_s.at[1])
    for k in range(1, nc):
        left(wog.at[core], oc_s.at[k])
        left(xg.at[pl.ds(0, ny)], xc_s.at[k])
    for i in range(1, ny):
        left(xg.at[me], xy_s.at[i])
    left(idg.at[pl.ds(0, n - 1)], id_s)
    for h in range(parts):
        left(ag.at[h, pl.ds(0, n - 1)], at_s.at[h])


def put_kernel(mixed_ref, codes_ref, ent_ref, mixed_out, codes_out, ent_out, sems):
    pairs = ((mixed_ref, mixed_out), (codes_ref, codes_out), (ent_ref, ent_out))
    copies = [pltpu.make_async_copy(src, dst, sems.at[i]) for i, (src, dst) in enumerate(pairs)]
    for c in copies:
        c.start()
    for c in copies:
        c.wait()


def on_device(
    cfg,
    residual_tiles,
    picture_label_tile,
    prenorm_multiplier,
    triple_projector,
    logit_scaling,
    final_projector,
    binarizer_projector,
    binarizer_offset,
):
    nz, nx, ny, nc = cfg["nz"], cfg["nx"], cfg["ny"], cfg["nc"]
    n, ndp = ny * nc, nz * nx
    _, rows, width = residual_tiles.shape
    heads_all = logit_scaling.shape[0]
    bits = binarizer_projector.shape[1]
    cols = width // n
    shard = triple_projector.shape[0]
    seq_len = rows * n
    parts = cols // LANES if cols % LANES == 0 else 1
    pc, sub = cols // parts, width // (nc * ny)
    quarters = 4 if rows % 128 == 0 else 1
    cfg = dict(
        cfg,
        heads=heads_all // n,
        channel=width // heads_all,
        q_block=min(256, rows),
        parts=parts,
        quarters=quarters,
    )
    dma = pltpu.SemaphoreType.DMA
    vmem, hbm = pl.BlockSpec(memory_space=pltpu.VMEM), pl.BlockSpec(memory_space=pl.ANY)
    bf16, f32 = jnp.bfloat16, jnp.float32
    mixed, codes, ent = pl.pallas_call(
        functools.partial(layer_kernel, cfg),
        out_shape=(
            pltpu.VMEM((rows, width), bf16),
            pltpu.VMEM((bits, 1, rows), f32),
            pltpu.VMEM((1, bits), f32),
        ),
        in_specs=[hbm] * 8,
        out_specs=(vmem, vmem, vmem),
        scratch_shapes=[
            pltpu.VMEM((parts, width, 3 * pc), bf16),
            pltpu.VMEM((nc, ny, width, sub), bf16),
            pltpu.VMEM((n, rows, width), bf16),
            pltpu.VMEM((n, 1, rows), jnp.int32),
            pltpu.VMEM((seq_len, width), bf16),
            pltpu.VMEM((parts, seq_len, pc + LANES), bf16),
            pltpu.VMEM((parts, seq_len, pc + LANES), bf16),
            pltpu.VMEM((parts, seq_len, 2 * pc), bf16),
            pltpu.VMEM((parts, n, rows, pc), bf16),
            pltpu.VMEM((parts, n, rows, pc), bf16),
            pltpu.VMEM((n * ndp, 1, LANES), f32),
            pltpu.VMEM((1, width), f32),
            pltpu.SMEM((heads_all,), f32),
            pltpu.VMEM((bits, width), bf16),
            pltpu.VMEM((1, bits), f32),
            dma((8,)),
            dma((2,)),
            dma((parts, nz)),
            dma((parts,)),
            dma((parts,)),
            dma((2,)),
            dma((nz,)),
            dma((2,)),
            dma((nz, nx)),
            dma((ny,)),
            dma((max(1, nz - 2), nx, ny)),
            dma((nc,)),
            dma((nc,)),
            dma((ny,)),
            dma((quarters, ny)),
            dma((nc,)),
            dma((nc,)),
            dma((quarters, max(1, ny - 1), nc)),
            dma(()),
            dma(()),
            dma((parts,)),
            dma((parts,)),
            dma(()),
            dma(()),
        ],
        compiler_params=pltpu.CompilerParams(
            collective_id=0, has_side_effects=True, vmem_limit_bytes=56 * 1024 * 1024
        ),
        name="layer",
    )(
        residual_tiles[0],
        picture_label_tile,
        prenorm_multiplier[None],
        triple_projector,
        logit_scaling,
        final_projector,
        binarizer_projector.T,
        binarizer_offset[None],
    )
    mixed, codes, ent = pl.pallas_call(
        put_kernel,
        out_shape=(
            jax.ShapeDtypeStruct((rows, width), bf16),
            jax.ShapeDtypeStruct((bits, 1, rows), f32),
            jax.ShapeDtypeStruct((1, bits), f32),
        ),
        in_specs=[vmem] * 3,
        out_specs=[hbm] * 3,
        scratch_shapes=[dma((3,))],
        name="put",
    )(*(pltpu.with_memory_space_constraint(v, pltpu.VMEM) for v in (mixed, codes, ent)))
    return mixed[None], jnp.swapaxes(codes, 0, 1), ent[0]


def solution(mesh):
    ndp, n = mesh.shape["dp"], mesh.shape["seq"]
    nx = math.isqrt(ndp // 2)
    if nx < 1 or ndp % nx:
        nx = 1
    nc = 2 if n % 2 == 0 else 1
    cfg = {"nz": ndp // nx, "nx": nx, "ny": n // nc, "nc": nc}
    return jax.shard_map(
        functools.partial(on_device, cfg),
        mesh=mesh,
        in_specs=(
            P("dp", "seq", None),
            P("dp", "seq"),
            P(),
            P("dp", None),
            P(),
            P("dp", None),
            P(),
            P(),
        ),
        out_specs=(P("dp", "seq", None), P("dp", None, "seq"), P()),
        check_vma=False,
    )
```

```python
import functools
import math

import jax
import jax.numpy as jnp
from jax import lax
from jax.experimental import pallas as pl
from jax.experimental.pallas import tpu as pltpu
from jax.sharding import PartitionSpec as P

EPS = 1e-06
MESH = pl.DeviceIdType.MESH
LANES = 128
SAME = 640.0


def layer_kernel(
    cfg,
    x_ref,
    ids_ref,
    gain_hbm,
    w_ref,
    scale_hbm,
    wo_ref,
    bits_hbm,
    off_hbm,
    mixed_ref,
    codes_ref,
    ent_ref,
    wg,
    wog,
    xg,
    idg,
    normed,
    qs,
    ks,
    vs,
    ao,
    ag,
    stats,
    gain_ref,
    scale_ref,
    bits_ref,
    off_ref,
    local_sem,
    wz_s,
    wz_r,
    wx_s,
    wx_r,
    oz_s,
    oz_r,
    ox_s,
    ox_r,
    oy_s,
    oy_r,
    oc_s,
    oc_r,
    xy_s,
    xy_r,
    xc_s,
    own_r,
    xc_r,
    id_s,
    id_r,
    at_s,
    at_r,
    st_s,
    st_r,
):
    nz, nx, ny, nc = cfg["nz"], cfg["nx"], cfg["ny"], cfg["nc"]
    n = ny * nc
    ndp = nz * nx
    heads, channel = cfg["heads"], cfg["channel"]
    parts, quarters = cfg["parts"], cfg["quarters"]
    rows, width = x_ref.shape
    shard = w_ref.shape[0]
    cols = width // n
    pc = cols // parts
    sub = width // (nc * ny)
    seq_len = rows * n
    bits = bits_ref.shape[0]
    dp = lax.axis_index("dp")
    me = lax.axis_index("seq")
    z = dp // nx
    x = dp % nx
    y = me // nc
    core = me % nc

    def dp_at(zz, xx):
        return zz * nx + xx

    def seq_at(yy, cc):
        return yy * nc + cc

    def remote(src, dst, ss, rs, d, s):
        return pltpu.make_async_remote_copy(
            src_ref=src, dst_ref=dst, send_sem=ss, recv_sem=rs, device_id=(d, s), device_id_type=MESH
        )

    def arrive(slot, sem):
        remote(slot, slot, sem, sem, dp, me).wait_recv()

    def left(slot, sem):
        remote(slot, slot, sem, sem, dp, me).wait_send()

    def shard_rows(zz, xx):
        return pl.ds(pl.multiple_of(dp_at(zz, xx) * shard, shard), shard)

    def w_slot_of(h):
        return lambda zz, xx: wg.at[h, shard_rows(zz, xx), :]

    w_slots = [w_slot_of(h) for h in range(parts)]
    x_rows = rows // quarters

    def x_piece(member, q):
        return xg.at[member, pl.ds(q * x_rows, x_rows), :]

    def o_slot(zz, xx):
        return wog.at[core, :, shard_rows(zz, xx), :]

    def o_sub(yy, zz, xx):
        return wog.at[core, yy, shard_rows(zz, xx), :]

    lo = jnp.minimum(z, nz - 1 - z)

    def piece(i):
        near = z - (i + 1) // 2 if i % 2 else z + (i + 1) // 2
        far = jnp.where(z > nz - 1 - z, z - (i - lo), z + (i - lo))
        return jnp.where(i <= 2 * lo, near, far) if i else z

    def line_start(slot, ss, rs, i, when=True):
        if nz == 1:
            return
        p = piece(i)
        here = slot(p, x)
        to_left = remote(here, here, ss.at[0], rs.at[p], dp_at(jnp.maximum(z - 1, 0), x), me)
        to_right = remote(here, here, ss.at[1], rs.at[p], dp_at(jnp.minimum(z + 1, nz - 1), x), me)
        for wanted, hop in (
            (jnp.logical_and(p >= z, z > 0), to_left),
            (jnp.logical_and(p <= z, z < nz - 1), to_right),
        ):

            @pl.when(wanted if when is True else jnp.logical_and(wanted, when))
            def _(hop=hop):
                hop.start()

    def line_left(block, ss):
        for zz in range(nz if nz > 1 else 0):

            @pl.when(z == zz)
            def _(zz=zz):
                if zz > 0:
                    left(block(nz - zz), ss.at[0])
                if zz < nz - 1:
                    left(block(zz + 1), ss.at[1])

    def across(slot, ss, rs, i):
        p = piece(i)
        for k in range(1, nx):
            remote(slot(p, x), slot(p, x), ss, rs(k), dp_at(z, (x + k) % nx), me).start()

    def share(here):
        for k in range(1, nc):
            remote(here, here, oc_s.at[k - 1], oc_r.at[k - 1], dp, seq_at(y, (core + k) % nc)).start()

    def whole(i):
        return i >= nz - 2 or ny == 1

    def o_crossing(i, k, d):
        p, xx = piece(i), (x - k + nx) % nx
        return o_slot(p, xx) if whole(i) else o_sub((y - d + ny) % ny, p, xx)

    def o_line_start(i, when=True):
        line_start(o_slot, oz_s, oz_r, i, when)

    def o_cross(i):
        slot = o_slot if whole(i) else lambda zz, xx: o_sub(y, zz, xx)
        across(slot, ox_s.at[int(whole(i))], lambda k: ox_r.at[i, k - 1], i)

    def o_line(i):
        p = piece(i)
        arrive(o_slot(p, x), oz_r.at[p])
        o_line_start(i)
        o_cross(i)
        share(o_slot(p, x))

    def o_crossed(i):
        for k in range(1, nx):
            here = o_crossing(i, k, 0)
            arrive(here, ox_r.at[i, k - 1])
            if not whole(i):
                for d in range(1, ny):
                    remote(
                        here, here, oy_s.at[d - 1], oy_r.at[i, k - 1, d - 1], dp, seq_at((y + d) % ny, core)
                    ).start()
            share(here)

    def o_last(i):
        for k in range(1, nx):
            for d in range(1, 1 if whole(i) else ny):
                arrive(o_crossing(i, k, d), oy_r.at[i, k - 1, d - 1])
                share(o_crossing(i, k, d))

    def o_shared():
        for k in range(1, nc):
            arrive(wog.at[(core - k + nc) % nc], oc_r.at[k - 1])

    barrier = pltpu.get_barrier_semaphore()

    def greet(d, s):
        pl.semaphore_signal(barrier, inc=1, device_id=(d, s), device_id_type=MESH)

    for i in range(1, n):
        greet(dp, (me + i) % n)
    for k in range(1, nx):
        greet(dp_at(z, (x + k) % nx), me)

    @pl.when(z > 0)
    def _():
        greet(dp_at(z - 1, x), me)

    @pl.when(z < nz - 1)
    def _():
        greet(dp_at(z + 1, x), me)

    own_w, own_o = [], []
    for h in range(parts):
        for part in range(3):
            own_w.append(
                pltpu.make_async_copy(
                    w_ref.at[:, pl.ds(pl.multiple_of(part * width + me * cols + h * pc, LANES), pc)],
                    wg.at[h, shard_rows(z, x), pl.ds(part * pc, pc)],
                    local_sem.at[8 + h],
                )
            )
    own_x = pltpu.make_async_copy(x_ref, xg.at[me], local_sem.at[1])
    own_id = pltpu.make_async_copy(ids_ref, idg.at[me], local_sem.at[2])
    for yy in range(ny):
        own_o.append(
            pltpu.make_async_copy(
                wo_ref.at[:, pl.ds(pl.multiple_of((core * ny + yy) * sub, LANES), sub)],
                o_sub(yy, z, x),
                local_sem.at[3],
            )
        )
    own_small = [
        pltpu.make_async_copy(src, dst, local_sem.at[4 + i])
        for i, (src, dst) in enumerate(
            ((gain_hbm, gain_ref), (scale_hbm, scale_ref), (bits_hbm, bits_ref), (off_hbm, off_ref))
        )
    ]
    for c in own_w + [own_id, own_x] + own_small + own_o:
        c.start()

    ends = jnp.where(z > 0, 1, 0) + jnp.where(z < nz - 1, 1, 0)
    pl.semaphore_wait(barrier, n - 1 + nx - 1 + ends)

    def w_along(i, h, when=True):
        line_start(w_slots[h], wz_s, wz_r.at[h], i, when)

    def w_across(i, h):
        across(w_slots[h], wx_s.at[h], lambda k: wx_r.at[h], i)

    for h in range(parts):
        own_block = w_slots[h](z, x)
        pltpu.make_async_copy(own_block, own_block, local_sem.at[8 + h]).wait()
        w_along(0, h, True if h == 0 else lo == 0)
        w_across(0, h)
    own_id.wait()
    for i in range(1, n):
        remote(idg.at[me], idg.at[me], id_s, id_r, dp, (me + i) % n).start()
    own_x.wait()
    for q in range(quarters):
        for i in range(1, ny):
            mine = x_piece(me, q)
            remote(mine, mine, xy_s.at[i - 1], xy_r.at[q, i - 1], dp, seq_at((y + i) % ny, core)).start()
    for k in range(1, nc):
        remote(xg.at[me], xg.at[me], xc_s.at[k - 1], own_r.at[k - 1], dp, seq_at(y, (core + k) % nc)).start()

    for c in own_small:
        c.wait()
    own_block = o_slot(z, x)
    pltpu.make_async_copy(own_block, own_block, local_sem.at[3]).wait()
    o_line_start(0, lo == 0)

    gain = gain_ref[...]
    block = math.gcd(x_rows, 64)

    def norm_rows(member, q, count=1):
        start = pl.multiple_of(member * rows, rows)

        def body(b, _):
            r0 = pl.multiple_of(q * x_rows + b * block, block)
            wide = xg[member, pl.ds(r0, block), :].astype(jnp.float32)
            ms = jnp.mean(wide * wide, axis=-1, keepdims=True)
            out = (wide * lax.rsqrt(ms + EPS) * gain).astype(jnp.bfloat16)
            normed[pl.ds(start + r0, block), :] = out
            return 0

        lax.fori_loop(0, count * x_rows // block, body, 0)

    norm_rows(me, 0, quarters)
    arrive(idg.at[pl.ds(0, n - 1)], id_r)
    lane_ids = lax.broadcasted_iota(jnp.int32, (rows, LANES), 1).astype(jnp.float32)
    for m in range(n):
        column = jnp.transpose(jnp.broadcast_to(idg[m].astype(jnp.float32), (LANES, rows)))
        hot = jnp.where(column == lane_ids, 1.0, 0.0)
        r = pl.ds(m * rows, rows)
        for h in range(parts):
            qs[h, r, pc:] = (hot * SAME).astype(jnp.bfloat16)
            ks[h, r, pc:] = hot.astype(jnp.bfloat16)
            vs[h, r, pc:] = jnp.ones((rows, pc), jnp.bfloat16)
    for k in range(1, nc):
        other = seq_at(y, (core - k + nc) % nc)
        arrive(xg.at[other], own_r.at[k - 1])
        norm_rows(other, 0, quarters)

    def x_arrived(i, q):
        source = seq_at((y - i + ny) % ny, core)
        slot = x_piece(source, q)
        arrive(slot, xy_r.at[q, i - 1])
        for k in range(1, nc):
            remote(slot, slot, xc_s.at[k - 1], xc_r.at[q, i - 1, k - 1], dp, seq_at(y, (core + k) % nc)).start()
        norm_rows(source, q)

    def x_shared(i, q):
        for k in range(1, nc):
            other = seq_at((y - i + ny) % ny, (core - k + nc) % nc)
            arrive(x_piece(other, q), xc_r.at[q, i - 1, k - 1])
            norm_rows(other, q)

    def w_arrived(i, h):
        arrive(w_slots[h](piece(i), x), wz_r.at[h, piece(i)])
        w_along(i, h)
        w_across(i, h)
        if (i, h) == (min(2, nz - 1), 0):
            for later in range(1, parts):
                w_along(0, later, lo > 0)

    events = []
    for i in range(1, nz):
        for h in range(parts):
            events.append(((h * (nz - 1) + i) * shard * 3 * pc, 0, i, h))
    for i in range(1, ny):
        for q in range(quarters):
            events.append((((i - 1) * quarters + q + 1) * x_rows * width, 1, i, q))
    waiting = []
    for _, stream, i, j in sorted(events):
        if stream == 0:
            w_arrived(i, j)
        else:
            x_arrived(i, j)
            waiting.append((i, j))
            if len(waiting) > 1:
                x_shared(*waiting.pop(0))
    o_line_start(0, lo > 0)
    o_cross(0)
    share(o_slot(z, x))
    for late in waiting:
        x_shared(*late)

    row_block = 256
    blocks = seq_len // row_block

    def group_of(shape, dim):
        return lax.div(lax.broadcasted_iota(jnp.int32, shape, dim), jnp.int32(channel))

    pair = (2 * pc, 2 * pc)
    same_head = jnp.where(group_of(pair, 0) == group_of(pair, 1), 1.0, 0.0).astype(jnp.bfloat16)
    part_heads = pc // channel
    last = parts - 1

    def project(h):
        scale_row = jnp.ones((1, 2 * pc), jnp.float32)
        for g in range(part_heads):
            value = scale_ref[me * heads + h * part_heads + g] / math.sqrt(channel)
            scale_row = jnp.where(group_of((1, 2 * pc), 1) == g, value, scale_row)
        if nx > 1:
            arrive(wg.at[h, pl.ds(0, nz * (nx - 1) * shard), :], wx_r.at[h])

        for b in range(blocks):
            r = pl.ds(b * row_block, row_block)
            joined = jnp.dot(normed[r, :], wg[h], preferred_element_type=jnp.float32).astype(jnp.bfloat16)
            qk = joined[:, : 2 * pc].astype(jnp.float32)
            square = qk * qk
            high = square.astype(jnp.bfloat16)
            low = (square - high.astype(jnp.float32)).astype(jnp.bfloat16)
            total = jnp.dot(high, same_head, preferred_element_type=jnp.float32) + jnp.dot(
                low, same_head, preferred_element_type=jnp.float32
            )
            qk = (qk * lax.rsqrt(total / channel + EPS) * scale_row).astype(jnp.bfloat16)
            qs[h, r, :pc] = qk[:, :pc]
            ks[h, r, :pc] = qk[:, pc:]
            vs[h, r, :pc] = joined[:, 2 * pc :]

    q_block = cfg["q_block"]
    lane_head = group_of((q_block, pc), 1)

    def stage_target(t, sign):
        dy = (t // nc + 1) % ny
        dc = (t + 1) % nc
        if sign > 0:
            return seq_at((y + dy) % ny, (core + dc) % nc)
        return seq_at((y - dy + ny) % ny, (core - dc + nc) % nc)

    def a2a(h, t):
        j = stage_target(t, 1)
        return remote(ao.at[h, j], ag.at[h, me], at_s.at[h], at_r.at[h], dp, j)

    def attend(h, stages):
        for t in stages:
            j = stage_target(t, 1)
            for part in range(rows // q_block):
                r = pl.ds(pl.multiple_of(j * rows + part * q_block, q_block), q_block)
                qb = qs[h, r, :]
                out = jnp.zeros((q_block, pc), jnp.float32)
                for g in range(part_heads):
                    mine = lane_head == g
                    qh = jnp.concatenate([jnp.where(mine, qb[:, :pc], jnp.zeros_like(qb[:, :pc])), qb[:, pc:]], axis=1)
                    s = lax.dot_general(qh, ks[h], (((1,), (1,)), ((), ())), preferred_element_type=jnp.float32)
                    p = jnp.exp(s - jnp.max(s, axis=-1, keepdims=True))
                    o = jnp.dot(p.astype(jnp.bfloat16), vs[h], preferred_element_type=jnp.float32)
                    out = jnp.where(mine, o[:, :pc] / o[:, pc:], out)
                ao[h, j, pl.ds(part * q_block, q_block), :] = out.astype(jnp.bfloat16)
        for t in stages:
            if t < n - 1:
                a2a(h, t).start()

    half = n // 2
    for h in range(last):
        project(h)
        attend(h, range(n))
    for i in range(1, nz - 1):
        o_line(i)
    o_crossed(0)
    project(last)
    for t in range(half):
        attend(last, (t,))
    if nz > 1:
        o_crossed(1)
        o_line(nz - 1)
    attend(last, range(half, n))
    for i in range(2, nz):
        o_crossed(i)
        o_last(i - 2)
    for i in range(max(0, nz - 2), nz):
        o_last(i)
    for h in range(parts):
        arrive(ag.at[h, pl.ds(0, n - 1)], at_r.at[h])
        ag[h, me] = ao[h, me]

    attention = jnp.concatenate([ag[h, m] for m in range(n) for h in range(parts)], axis=1)
    for g in range(nc):
        if g == 1:
            o_shared()
        half = (core + g) % nc
        for yy in range(ny):
            lanes = pl.ds(pl.multiple_of((half * ny + yy) * sub, LANES), sub)
            prod = jnp.dot(attention, wog[half, yy], preferred_element_type=jnp.float32)
            mixed_ref[:, lanes] = (xg[me, :, lanes].astype(jnp.float32) + prod).astype(jnp.bfloat16)

    logits = lax.dot_general(
        bits_ref[...], mixed_ref[...], (((1,), (1,)), ((), ())), preferred_element_type=jnp.float32
    )
    eye = lax.broadcasted_iota(jnp.int32, (bits, bits), 0) == lax.broadcasted_iota(
        jnp.int32, (bits, bits), 1
    )
    offset = jnp.sum(jnp.where(eye, off_ref[...], 0.0), axis=1, keepdims=True)
    probs = jax.nn.sigmoid(4.0 * (logits + offset))
    lanes_eye = lax.broadcasted_iota(jnp.int32, (bits, LANES), 0) == lax.broadcasted_iota(
        jnp.int32, (bits, LANES), 1
    )
    own_sums = jnp.sum(probs, axis=1, keepdims=True)
    count = n * ndp
    mine = dp * n + me
    stats[mine, :, :] = jnp.sum(jnp.where(lanes_eye, own_sums, 0.0), axis=0, keepdims=True)

    def tell(i, _):
        zz = jnp.where(2 * z < nz, nz - 1 - i, i)
        for k in range(nx):
            for m in range(n):
                there = remote(
                    stats.at[mine], stats.at[mine], st_s, st_r, dp_at(zz, (x + k) % nx), (me + m) % n
                )
                if k or m:
                    there.start()
                else:
                    pl.when(zz != z)(there.start)
        return 0

    lax.fori_loop(0, nz, tell, 0)
    others = stats.at[pl.ds(0, count - 1)]
    arrive(others, st_r)
    total = jnp.sum(stats[...], axis=0)
    marginal = total / (seq_len * ndp)
    line = marginal[:, :bits]
    ent_ref[...] = -(line * jnp.log(line) + (1.0 - line) * jnp.log(1.0 - line))
    codes = probs - jnp.sum(jnp.where(lanes_eye, marginal, 0.0), axis=1, keepdims=True)
    for b in range(bits):
        codes_ref[b] = codes[b : b + 1, :]

    left(others, st_s)
    line_left(lambda m: wg.at[:, pl.ds(0, m * shard), :], wz_s)
    line_left(lambda m: wog.at[0, :, pl.ds(0, m * shard), :], oz_s)
    halves = [i for i in range(nz) if not whole(i)]
    if nx > 1:
        for h in range(parts):
            left(wg.at[h, pl.ds(0, nz * (nx - 1) * shard), :], wx_s.at[h])
        if halves:
            block = wog.at[0, 0, pl.ds(0, len(halves) * (nx - 1) * shard), :]
            left(block, ox_s.at[0])
            for d in range(1, ny):
                left(block, oy_s.at[d - 1])
        if len(halves) < nz:
            left(wog.at[0, :, pl.ds(0, (nz - len(halves)) * (nx - 1) * shard), :], ox_s.at[1])
    for k in range(1, nc):
        left(wog.at[core], oc_s.at[k - 1])
        left(xg.at[pl.ds(0, ny)], xc_s.at[k - 1])
    for i in range(1, ny):
        left(xg.at[me], xy_s.at[i - 1])
    left(idg.at[pl.ds(0, n - 1)], id_s)
    for h in range(parts):
        left(ag.at[h, pl.ds(0, n - 1)], at_s.at[h])


def put_kernel(mixed_ref, codes_ref, ent_ref, mixed_out, codes_out, ent_out, sems):
    pairs = ((mixed_ref, mixed_out), (codes_ref, codes_out), (ent_ref, ent_out))
    copies = [pltpu.make_async_copy(src, dst, sems.at[i]) for i, (src, dst) in enumerate(pairs)]
    for c in copies:
        c.start()
    for c in copies:
        c.wait()


def on_device(
    cfg,
    residual_tiles,
    picture_label_tile,
    prenorm_multiplier,
    triple_projector,
    logit_scaling,
    final_projector,
    binarizer_projector,
    binarizer_offset,
):
    nz, nx, ny, nc = cfg["nz"], cfg["nx"], cfg["ny"], cfg["nc"]
    n, ndp = ny * nc, nz * nx
    _, rows, width = residual_tiles.shape
    heads_all = logit_scaling.shape[0]
    bits = binarizer_projector.shape[1]
    cols = width // n
    shard = triple_projector.shape[0]
    seq_len = rows * n
    parts = cols // LANES if cols % LANES == 0 else 1
    pc, sub = cols // parts, width // (nc * ny)
    quarters = 4 if rows % 128 == 0 else 1
    cfg = dict(
        cfg,
        heads=heads_all // n,
        channel=width // heads_all,
        q_block=min(256, rows),
        parts=parts,
        quarters=quarters,
    )
    dma = pltpu.SemaphoreType.DMA
    vmem, hbm = pl.BlockSpec(memory_space=pltpu.VMEM), pl.BlockSpec(memory_space=pl.ANY)
    bf16, f32 = jnp.bfloat16, jnp.float32
    ox, oy, oc = max(1, nx - 1), max(1, ny - 1), max(1, nc - 1)
    mixed, codes, ent = pl.pallas_call(
        functools.partial(layer_kernel, cfg),
        out_shape=(
            pltpu.VMEM((rows, width), bf16),
            pltpu.VMEM((bits, 1, rows), f32),
            pltpu.VMEM((1, bits), f32),
        ),
        in_specs=[hbm] * 8,
        out_specs=(vmem, vmem, vmem),
        scratch_shapes=[
            pltpu.VMEM((parts, width, 3 * pc), bf16),
            pltpu.VMEM((nc, ny, width, sub), bf16),
            pltpu.VMEM((n, rows, width), bf16),
            pltpu.VMEM((n, 1, rows), jnp.int32),
            pltpu.VMEM((seq_len, width), bf16),
            pltpu.VMEM((parts, seq_len, pc + LANES), bf16),
            pltpu.VMEM((parts, seq_len, pc + LANES), bf16),
            pltpu.VMEM((parts, seq_len, 2 * pc), bf16),
            pltpu.VMEM((parts, n, rows, pc), bf16),
            pltpu.VMEM((parts, n, rows, pc), bf16),
            pltpu.VMEM((n * ndp, 1, LANES), f32),
            pltpu.VMEM((1, width), f32),
            pltpu.SMEM((heads_all,), f32),
            pltpu.VMEM((bits, width), bf16),
            pltpu.VMEM((1, bits), f32),
            dma((8 + parts,)),
            dma((2,)),
            dma((parts, nz)),
            dma((parts,)),
            dma((parts,)),
            dma((2,)),
            dma((nz,)),
            dma((2,)),
            dma((nz, ox)),
            dma((oy,)),
            dma((max(1, nz - 2), ox, oy)),
            dma((oc,)),
            dma((oc,)),
            dma((oy,)),
            dma((quarters, oy)),
            dma((oc,)),
            dma((oc,)),
            dma((quarters, oy, oc)),
            dma(()),
            dma(()),
            dma((parts,)),
            dma((parts,)),
            dma(()),
            dma(()),
        ],
        compiler_params=pltpu.CompilerParams(
            collective_id=0, has_side_effects=True, vmem_limit_bytes=56 * 1024 * 1024
        ),
        name="layer",
    )(
        residual_tiles[0],
        picture_label_tile,
        prenorm_multiplier[None],
        triple_projector,
        logit_scaling,
        final_projector,
        binarizer_projector.T,
        binarizer_offset[None],
    )
    mixed, codes, ent = pl.pallas_call(
        put_kernel,
        out_shape=(
            jax.ShapeDtypeStruct((rows, width), bf16),
            jax.ShapeDtypeStruct((bits, 1, rows), f32),
            jax.ShapeDtypeStruct((1, bits), f32),
        ),
        in_specs=[vmem] * 3,
        out_specs=[hbm] * 3,
        scratch_shapes=[dma((3,))],
        name="put",
    )(*(pltpu.with_memory_space_constraint(v, pltpu.VMEM) for v in (mixed, codes, ent)))
    return mixed[None], jnp.swapaxes(codes, 0, 1), ent[0]


def solution(mesh):
    ndp, n = mesh.shape["dp"], mesh.shape["seq"]
    nx = math.isqrt(ndp // 2)
    if nx < 1 or ndp % nx:
        nx = 1
    nc = 2 if n % 2 == 0 else 1
    cfg = {"nz": ndp // nx, "nx": nx, "ny": n // nc, "nc": nc}
    return jax.shard_map(
        functools.partial(on_device, cfg),
        mesh=mesh,
        in_specs=(
            P("dp", "seq", None),
            P("dp", "seq"),
            P(),
            P("dp", None),
            P(),
            P("dp", None),
            P(),
            P(),
        ),
        out_specs=(P("dp", "seq", None), P("dp", None, "seq"), P()),
        check_vma=False,
    )
```

```python
import functools
import math

import jax
import jax.numpy as jnp
from jax import lax
from jax.experimental import pallas as pl
from jax.experimental.pallas import tpu as pltpu
from jax.sharding import PartitionSpec as P

EPS = 1e-06
MESH = pl.DeviceIdType.MESH
LANES = 128
SAME = 640.0


def layer_kernel(
    cfg,
    x_ref,
    ids_ref,
    gain_hbm,
    w_ref,
    scale_hbm,
    wo_ref,
    bits_hbm,
    off_hbm,
    mixed_ref,
    codes_ref,
    ent_ref,
    wg,
    wog,
    xg,
    idg,
    normed,
    qs,
    ks,
    vs,
    ao,
    ag,
    stats,
    gain_ref,
    scale_ref,
    bits_ref,
    off_ref,
    local_sem,
    wz_s,
    wz_r,
    wx_s,
    wx_r,
    oz_s,
    oz_r,
    ox_s,
    ox_r,
    oy_s,
    oy_r,
    oc_s,
    oc_r,
    xy_s,
    xy_r,
    xc_s,
    own_r,
    xc_r,
    id_s,
    id_r,
    at_s,
    at_r,
    st_s,
    st_r,
):
    nz, nx, ny, nc = cfg["nz"], cfg["nx"], cfg["ny"], cfg["nc"]
    n = ny * nc
    ndp = nz * nx
    heads, channel = cfg["heads"], cfg["channel"]
    parts, quarters = cfg["parts"], cfg["quarters"]
    rows, width = x_ref.shape
    shard = w_ref.shape[0]
    cols = width // n
    pc = cols // parts
    sub = width // (nc * ny)
    seq_len = rows * n
    bits = bits_ref.shape[0]
    dp = lax.axis_index("dp")
    me = lax.axis_index("seq")
    z = dp // nx
    x = dp % nx
    y = me // nc
    core = me % nc

    def dp_at(zz, xx):
        return zz * nx + xx

    def seq_at(yy, cc):
        return yy * nc + cc

    def remote(src, dst, ss, rs, d, s):
        return pltpu.make_async_remote_copy(
            src_ref=src, dst_ref=dst, send_sem=ss, recv_sem=rs, device_id=(d, s), device_id_type=MESH
        )

    def arrive(slot, sem):
        remote(slot, slot, sem, sem, dp, me).wait_recv()

    def left(slot, sem):
        remote(slot, slot, sem, sem, dp, me).wait_send()

    def shard_rows(zz, xx):
        return pl.ds(pl.multiple_of(dp_at(zz, xx) * shard, shard), shard)

    def w_slot_of(h):
        return lambda zz, xx: wg.at[h, shard_rows(zz, xx), :]

    w_slots = [w_slot_of(h) for h in range(parts)]
    x_rows = rows // quarters

    def x_piece(member, q):
        return xg.at[member, pl.ds(q * x_rows, x_rows), :]

    def o_slot(zz, xx):
        return wog.at[core, :, shard_rows(zz, xx), :]

    def o_sub(yy, zz, xx):
        return wog.at[core, yy, shard_rows(zz, xx), :]

    lo = jnp.minimum(z, nz - 1 - z)

    def piece(i):
        near = z - (i + 1) // 2 if i % 2 else z + (i + 1) // 2
        far = jnp.where(z > nz - 1 - z, z - (i - lo), z + (i - lo))
        return jnp.where(i <= 2 * lo, near, far) if i else z

    def line_start(slot, ss, rs, i, when=True):
        if nz == 1:
            return
        p = piece(i)
        here = slot(p, x)
        to_left = remote(here, here, ss.at[0], rs.at[p], dp_at(jnp.maximum(z - 1, 0), x), me)
        to_right = remote(here, here, ss.at[1], rs.at[p], dp_at(jnp.minimum(z + 1, nz - 1), x), me)
        for wanted, hop in (
            (jnp.logical_and(p >= z, z > 0), to_left),
            (jnp.logical_and(p <= z, z < nz - 1), to_right),
        ):

            @pl.when(wanted if when is True else jnp.logical_and(wanted, when))
            def _(hop=hop):
                hop.start()

    def line_left(block, ss):
        for zz in range(nz if nz > 1 else 0):

            @pl.when(z == zz)
            def _(zz=zz):
                if zz > 0:
                    left(block(nz - zz), ss.at[0])
                if zz < nz - 1:
                    left(block(zz + 1), ss.at[1])

    def across(slot, ss, rs, i):
        p = piece(i)
        for k in range(1, nx):
            remote(slot(p, x), slot(p, x), ss, rs(k), dp_at(z, (x + k) % nx), me).start()

    def share(here):
        for k in range(1, nc):
            remote(here, here, oc_s.at[k - 1], oc_r.at[k - 1], dp, seq_at(y, (core + k) % nc)).start()

    def whole(i):
        return i >= nz - 2 or ny == 1

    def o_crossing(i, k, d):
        p, xx = piece(i), (x - k + nx) % nx
        return o_slot(p, xx) if whole(i) else o_sub((y - d + ny) % ny, p, xx)

    def o_line_start(i, when=True):
        line_start(o_slot, oz_s, oz_r, i, when)

    def o_cross(i):
        slot = o_slot if whole(i) else lambda zz, xx: o_sub(y, zz, xx)
        across(slot, ox_s.at[int(whole(i))], lambda k: ox_r.at[i, k - 1], i)

    def o_line(i):
        p = piece(i)
        arrive(o_slot(p, x), oz_r.at[p])
        o_line_start(i)
        o_cross(i)
        share(o_slot(p, x))

    def o_crossed(i):
        for k in range(1, nx):
            here = o_crossing(i, k, 0)
            arrive(here, ox_r.at[i, k - 1])
            if not whole(i):
                for d in range(1, ny):
                    remote(
                        here, here, oy_s.at[d - 1], oy_r.at[i, k - 1, d - 1], dp, seq_at((y + d) % ny, core)
                    ).start()
            share(here)

    def o_last(i):
        for k in range(1, nx):
            for d in range(1, 1 if whole(i) else ny):
                arrive(o_crossing(i, k, d), oy_r.at[i, k - 1, d - 1])
                share(o_crossing(i, k, d))

    def o_shared():
        for k in range(1, nc):
            arrive(wog.at[(core - k + nc) % nc], oc_r.at[k - 1])

    barrier = pltpu.get_barrier_semaphore()

    def greet(d, s):
        pl.semaphore_signal(barrier, inc=1, device_id=(d, s), device_id_type=MESH)

    for i in range(1, n):
        greet(dp, (me + i) % n)
    for k in range(1, nx):
        greet(dp_at(z, (x + k) % nx), me)

    @pl.when(z > 0)
    def _():
        greet(dp_at(z - 1, x), me)

    @pl.when(z < nz - 1)
    def _():
        greet(dp_at(z + 1, x), me)

    own_w, own_o = [], []
    for h in range(parts):
        for part in range(3):
            own_w.append(
                pltpu.make_async_copy(
                    w_ref.at[:, pl.ds(pl.multiple_of(part * width + me * cols + h * pc, LANES), pc)],
                    wg.at[h, shard_rows(z, x), pl.ds(part * pc, pc)],
                    local_sem.at[8 + h],
                )
            )
    own_x = pltpu.make_async_copy(x_ref, xg.at[me], local_sem.at[1])
    own_id = pltpu.make_async_copy(ids_ref, idg.at[me], local_sem.at[2])
    for yy in range(ny):
        own_o.append(
            pltpu.make_async_copy(
                wo_ref.at[:, pl.ds(pl.multiple_of((core * ny + yy) * sub, LANES), sub)],
                o_sub(yy, z, x),
                local_sem.at[3],
            )
        )
    own_small = [
        pltpu.make_async_copy(src, dst, local_sem.at[4 + i])
        for i, (src, dst) in enumerate(
            ((gain_hbm, gain_ref), (scale_hbm, scale_ref), (bits_hbm, bits_ref), (off_hbm, off_ref))
        )
    ]
    for c in own_w + [own_id, own_x] + own_small + own_o:
        c.start()

    ends = jnp.where(z > 0, 1, 0) + jnp.where(z < nz - 1, 1, 0)
    pl.semaphore_wait(barrier, n - 1 + nx - 1 + ends)

    def w_along(i, h, when=True):
        line_start(w_slots[h], wz_s, wz_r.at[h], i, when)

    def w_across(i, h):
        across(w_slots[h], wx_s.at[h], lambda k: wx_r.at[h], i)

    for h in range(parts):
        own_block = w_slots[h](z, x)
        pltpu.make_async_copy(own_block, own_block, local_sem.at[8 + h]).wait()
        w_along(0, h, True if h == 0 else lo == 0)
        w_across(0, h)
    own_id.wait()
    for i in range(1, n):
        remote(idg.at[me], idg.at[me], id_s, id_r, dp, (me + i) % n).start()
    own_x.wait()
    for q in range(quarters):
        for i in range(1, ny):
            mine = x_piece(me, q)
            remote(mine, mine, xy_s.at[i - 1], xy_r.at[q, i - 1], dp, seq_at((y + i) % ny, core)).start()
    for k in range(1, nc):
        remote(xg.at[me], xg.at[me], xc_s.at[k - 1], own_r.at[k - 1], dp, seq_at(y, (core + k) % nc)).start()

    for c in own_small:
        c.wait()
    own_block = o_slot(z, x)
    pltpu.make_async_copy(own_block, own_block, local_sem.at[3]).wait()
    o_line_start(0, lo == 0)

    gain = gain_ref[...]
    block = math.gcd(x_rows, 64)

    def norm_rows(member, q, count=1):
        start = pl.multiple_of(member * rows, rows)

        def body(b, _):
            r0 = pl.multiple_of(q * x_rows + b * block, block)
            wide = xg[member, pl.ds(r0, block), :].astype(jnp.float32)
            ms = jnp.mean(wide * wide, axis=-1, keepdims=True)
            out = (wide * lax.rsqrt(ms + EPS) * gain).astype(jnp.bfloat16)
            normed[pl.ds(start + r0, block), :] = out
            return 0

        lax.fori_loop(0, count * x_rows // block, body, 0)

    norm_rows(me, 0, quarters)
    arrive(idg.at[pl.ds(0, n - 1)], id_r)
    lane_ids = lax.broadcasted_iota(jnp.int32, (rows, LANES), 1).astype(jnp.float32)
    for m in range(n):
        column = jnp.transpose(jnp.broadcast_to(idg[m].astype(jnp.float32), (LANES, rows)))
        hot = jnp.where(column == lane_ids, 1.0, 0.0)
        r = pl.ds(m * rows, rows)
        for h in range(parts):
            qs[h, r, pc:] = (hot * SAME).astype(jnp.bfloat16)
            ks[h, r, pc:] = hot.astype(jnp.bfloat16)
            vs[h, r, pc:] = jnp.ones((rows, pc), jnp.bfloat16)
    for k in range(1, nc):
        other = seq_at(y, (core - k + nc) % nc)
        arrive(xg.at[other], own_r.at[k - 1])
        norm_rows(other, 0, quarters)

    def x_arrived(i, q):
        source = seq_at((y - i + ny) % ny, core)
        slot = x_piece(source, q)
        arrive(slot, xy_r.at[q, i - 1])
        for k in range(1, nc):
            remote(slot, slot, xc_s.at[k - 1], xc_r.at[q, i - 1, k - 1], dp, seq_at(y, (core + k) % nc)).start()
        norm_rows(source, q)

    def x_shared(i, q):
        for k in range(1, nc):
            other = seq_at((y - i + ny) % ny, (core - k + nc) % nc)
            arrive(x_piece(other, q), xc_r.at[q, i - 1, k - 1])
            norm_rows(other, q)

    def w_arrived(i, h):
        arrive(w_slots[h](piece(i), x), wz_r.at[h, piece(i)])
        w_along(i, h)
        w_across(i, h)
        if (i, h) == (min(2, nz - 1), 0):
            for later in range(1, parts):
                w_along(0, later, lo > 0)

    events = []
    for i in range(1, nz):
        for h in range(parts):
            events.append(((h * (nz - 1) + i) * shard * 3 * pc, 0, i, h))
    for i in range(1, ny):
        for q in range(quarters):
            events.append((((i - 1) * quarters + q + 1) * x_rows * width, 1, i, q))
    waiting = []
    for _, stream, i, j in sorted(events):
        if stream == 0:
            w_arrived(i, j)
        else:
            x_arrived(i, j)
            waiting.append((i, j))
            if len(waiting) > 1:
                x_shared(*waiting.pop(0))
    o_line_start(0, lo > 0)
    o_cross(0)
    share(o_slot(z, x))
    for late in waiting:
        x_shared(*late)

    row_block = 256
    blocks = seq_len // row_block

    def group_of(shape, dim):
        return lax.div(lax.broadcasted_iota(jnp.int32, shape, dim), jnp.int32(channel))

    pair = (2 * pc, 2 * pc)
    same_head = jnp.where(group_of(pair, 0) == group_of(pair, 1), 1.0, 0.0).astype(jnp.bfloat16)
    part_heads = pc // channel
    last = parts - 1

    def project(h):
        scale_row = jnp.ones((1, 2 * pc), jnp.float32)
        for g in range(part_heads):
            value = scale_ref[me * heads + h * part_heads + g] / math.sqrt(channel)
            scale_row = jnp.where(group_of((1, 2 * pc), 1) == g, value, scale_row)
        if nx > 1:
            arrive(wg.at[h, pl.ds(0, nz * (nx - 1) * shard), :], wx_r.at[h])

        for b in range(blocks):
            r = pl.ds(b * row_block, row_block)
            joined = jnp.dot(normed[r, :], wg[h], preferred_element_type=jnp.float32).astype(jnp.bfloat16)
            qk = joined[:, : 2 * pc].astype(jnp.float32)
            square = qk * qk
            high = square.astype(jnp.bfloat16)
            low = (square - high.astype(jnp.float32)).astype(jnp.bfloat16)
            total = jnp.dot(high, same_head, preferred_element_type=jnp.float32) + jnp.dot(
                low, same_head, preferred_element_type=jnp.float32
            )
            qk = (qk * lax.rsqrt(total / channel + EPS) * scale_row).astype(jnp.bfloat16)
            qs[h, r, :pc] = qk[:, :pc]
            ks[h, r, :pc] = qk[:, pc:]
            vs[h, r, :pc] = joined[:, 2 * pc :]

    q_block = cfg["q_block"]
    lane_head = group_of((q_block, pc), 1)

    def stage_target(t, sign):
        dy = (t // nc + 1) % ny
        dc = (t + 1) % nc
        if sign > 0:
            return seq_at((y + dy) % ny, (core + dc) % nc)
        return seq_at((y - dy + ny) % ny, (core - dc + nc) % nc)

    def a2a(h, t):
        j = stage_target(t, 1)
        return remote(ao.at[h, j], ag.at[h, me], at_s.at[h], at_r.at[h], dp, j)

    def attend(h, stages):
        for t in stages:
            j = stage_target(t, 1)
            for part in range(rows // q_block):
                r = pl.ds(pl.multiple_of(j * rows + part * q_block, q_block), q_block)
                qb = qs[h, r, :]
                out = jnp.zeros((q_block, pc), jnp.float32)
                for g in range(part_heads):
                    mine = lane_head == g
                    qh = jnp.concatenate([jnp.where(mine, qb[:, :pc], jnp.zeros_like(qb[:, :pc])), qb[:, pc:]], axis=1)
                    s = lax.dot_general(qh, ks[h], (((1,), (1,)), ((), ())), preferred_element_type=jnp.float32)
                    p = jnp.exp(s - jnp.max(s, axis=-1, keepdims=True))
                    o = jnp.dot(p.astype(jnp.bfloat16), vs[h], preferred_element_type=jnp.float32)
                    out = jnp.where(mine, o[:, :pc] / o[:, pc:], out)
                ao[h, j, pl.ds(part * q_block, q_block), :] = out.astype(jnp.bfloat16)
        for t in stages:
            if t < n - 1:
                a2a(h, t).start()

    half = n // 2
    for h in range(last):
        project(h)
        attend(h, range(n))
    for i in range(1, nz - 1):
        o_line(i)
    o_crossed(0)
    project(last)
    for t in range(half):
        attend(last, (t,))
    if nz > 1:
        o_crossed(1)
        o_line(nz - 1)
    for t in range(half, n):
        attend(last, (t,))
    for i in range(2, nz):
        o_crossed(i)
        o_last(i - 2)
    for i in range(max(0, nz - 2), nz):
        o_last(i)
    for h in range(parts):
        arrive(ag.at[h, pl.ds(0, n - 1)], at_r.at[h])
        ag[h, me] = ao[h, me]

    attention = jnp.concatenate([ag[h, m] for m in range(n) for h in range(parts)], axis=1)
    for g in range(nc):
        if g == 1:
            o_shared()
        half = (core + g) % nc
        for yy in range(ny):
            lanes = pl.ds(pl.multiple_of((half * ny + yy) * sub, LANES), sub)
            prod = jnp.dot(attention, wog[half, yy], preferred_element_type=jnp.float32)
            mixed_ref[:, lanes] = (xg[me, :, lanes].astype(jnp.float32) + prod).astype(jnp.bfloat16)

    logits = lax.dot_general(
        bits_ref[...], mixed_ref[...], (((1,), (1,)), ((), ())), preferred_element_type=jnp.float32
    )
    eye = lax.broadcasted_iota(jnp.int32, (bits, bits), 0) == lax.broadcasted_iota(
        jnp.int32, (bits, bits), 1
    )
    offset = jnp.sum(jnp.where(eye, off_ref[...], 0.0), axis=1, keepdims=True)
    probs = jax.nn.sigmoid(4.0 * (logits + offset))
    lanes_eye = lax.broadcasted_iota(jnp.int32, (bits, LANES), 0) == lax.broadcasted_iota(
        jnp.int32, (bits, LANES), 1
    )
    own_sums = jnp.sum(probs, axis=1, keepdims=True)
    count = n * ndp
    mine = dp * n + me
    stats[mine, :, :] = jnp.sum(jnp.where(lanes_eye, own_sums, 0.0), axis=0, keepdims=True)

    def tell(i, _):
        zz = jnp.where(2 * z < nz, nz - 1 - i, i)
        for k in range(nx):
            for m in range(n):
                there = remote(
                    stats.at[mine], stats.at[mine], st_s, st_r, dp_at(zz, (x + k) % nx), (me + m) % n
                )
                if k or m:
                    there.start()
                else:
                    pl.when(zz != z)(there.start)
        return 0

    lax.fori_loop(0, nz, tell, 0)
    others = stats.at[pl.ds(0, count - 1)]
    arrive(others, st_r)
    total = jnp.sum(stats[...], axis=0)
    marginal = total / (seq_len * ndp)
    line = marginal[:, :bits]
    ent_ref[...] = -(line * jnp.log(line) + (1.0 - line) * jnp.log(1.0 - line))
    codes = probs - jnp.sum(jnp.where(lanes_eye, marginal, 0.0), axis=1, keepdims=True)
    for b in range(bits):
        codes_ref[b] = codes[b : b + 1, :]

    left(others, st_s)
    line_left(lambda m: wg.at[:, pl.ds(0, m * shard), :], wz_s)
    line_left(lambda m: wog.at[0, :, pl.ds(0, m * shard), :], oz_s)
    halves = [i for i in range(nz) if not whole(i)]
    if nx > 1:
        for h in range(parts):
            left(wg.at[h, pl.ds(0, nz * (nx - 1) * shard), :], wx_s.at[h])
        if halves:
            block = wog.at[0, 0, pl.ds(0, len(halves) * (nx - 1) * shard), :]
            left(block, ox_s.at[0])
            for d in range(1, ny):
                left(block, oy_s.at[d - 1])
        if len(halves) < nz:
            left(wog.at[0, :, pl.ds(0, (nz - len(halves)) * (nx - 1) * shard), :], ox_s.at[1])
    for k in range(1, nc):
        left(wog.at[core], oc_s.at[k - 1])
        left(xg.at[pl.ds(0, ny)], xc_s.at[k - 1])
    for i in range(1, ny):
        left(xg.at[me], xy_s.at[i - 1])
    left(idg.at[pl.ds(0, n - 1)], id_s)
    for h in range(parts):
        left(ag.at[h, pl.ds(0, n - 1)], at_s.at[h])


def put_kernel(mixed_ref, codes_ref, ent_ref, mixed_out, codes_out, ent_out, sems):
    pairs = ((mixed_ref, mixed_out), (codes_ref, codes_out), (ent_ref, ent_out))
    copies = [pltpu.make_async_copy(src, dst, sems.at[i]) for i, (src, dst) in enumerate(pairs)]
    for c in copies:
        c.start()
    for c in copies:
        c.wait()


def on_device(
    cfg,
    residual_tiles,
    picture_label_tile,
    prenorm_multiplier,
    triple_projector,
    logit_scaling,
    final_projector,
    binarizer_projector,
    binarizer_offset,
):
    nz, nx, ny, nc = cfg["nz"], cfg["nx"], cfg["ny"], cfg["nc"]
    n, ndp = ny * nc, nz * nx
    _, rows, width = residual_tiles.shape
    heads_all = logit_scaling.shape[0]
    bits = binarizer_projector.shape[1]
    cols = width // n
    shard = triple_projector.shape[0]
    seq_len = rows * n
    parts = cols // LANES if cols % LANES == 0 else 1
    pc, sub = cols // parts, width // (nc * ny)
    quarters = 4 if rows % 128 == 0 else 1
    cfg = dict(
        cfg,
        heads=heads_all // n,
        channel=width // heads_all,
        q_block=min(256, rows),
        parts=parts,
        quarters=quarters,
    )
    dma = pltpu.SemaphoreType.DMA
    vmem, hbm = pl.BlockSpec(memory_space=pltpu.VMEM), pl.BlockSpec(memory_space=pl.ANY)
    bf16, f32 = jnp.bfloat16, jnp.float32
    ox, oy, oc = max(1, nx - 1), max(1, ny - 1), max(1, nc - 1)
    mixed, codes, ent = pl.pallas_call(
        functools.partial(layer_kernel, cfg),
        out_shape=(
            pltpu.VMEM((rows, width), bf16),
            pltpu.VMEM((bits, 1, rows), f32),
            pltpu.VMEM((1, bits), f32),
        ),
        in_specs=[hbm] * 8,
        out_specs=(vmem, vmem, vmem),
        scratch_shapes=[
            pltpu.VMEM((parts, width, 3 * pc), bf16),
            pltpu.VMEM((nc, ny, width, sub), bf16),
            pltpu.VMEM((n, rows, width), bf16),
            pltpu.VMEM((n, 1, rows), jnp.int32),
            pltpu.VMEM((seq_len, width), bf16),
            pltpu.VMEM((parts, seq_len, pc + LANES), bf16),
            pltpu.VMEM((parts, seq_len, pc + LANES), bf16),
            pltpu.VMEM((parts, seq_len, 2 * pc), bf16),
            pltpu.VMEM((parts, n, rows, pc), bf16),
            pltpu.VMEM((parts, n, rows, pc), bf16),
            pltpu.VMEM((n * ndp, 1, LANES), f32),
            pltpu.VMEM((1, width), f32),
            pltpu.SMEM((heads_all,), f32),
            pltpu.VMEM((bits, width), bf16),
            pltpu.VMEM((1, bits), f32),
            dma((8 + parts,)),
            dma((2,)),
            dma((parts, nz)),
            dma((parts,)),
            dma((parts,)),
            dma((2,)),
            dma((nz,)),
            dma((2,)),
            dma((nz, ox)),
            dma((oy,)),
            dma((max(1, nz - 2), ox, oy)),
            dma((oc,)),
            dma((oc,)),
            dma((oy,)),
            dma((quarters, oy)),
            dma((oc,)),
            dma((oc,)),
            dma((quarters, oy, oc)),
            dma(()),
            dma(()),
            dma((parts,)),
            dma((parts,)),
            dma(()),
            dma(()),
        ],
        compiler_params=pltpu.CompilerParams(
            collective_id=0, has_side_effects=True, vmem_limit_bytes=56 * 1024 * 1024
        ),
        name="layer",
    )(
        residual_tiles[0],
        picture_label_tile,
        prenorm_multiplier[None],
        triple_projector,
        logit_scaling,
        final_projector,
        binarizer_projector.T,
        binarizer_offset[None],
    )
    mixed, codes, ent = pl.pallas_call(
        put_kernel,
        out_shape=(
            jax.ShapeDtypeStruct((rows, width), bf16),
            jax.ShapeDtypeStruct((bits, 1, rows), f32),
            jax.ShapeDtypeStruct((1, bits), f32),
        ),
        in_specs=[vmem] * 3,
        out_specs=[hbm] * 3,
        scratch_shapes=[dma((3,))],
        name="put",
    )(*(pltpu.with_memory_space_constraint(v, pltpu.VMEM) for v in (mixed, codes, ent)))
    return mixed[None], jnp.swapaxes(codes, 0, 1), ent[0]


def solution(mesh):
    ndp, n = mesh.shape["dp"], mesh.shape["seq"]
    nx = math.isqrt(ndp // 2)
    if nx < 1 or ndp % nx:
        nx = 1
    nc = 2 if n % 2 == 0 else 1
    cfg = {"nz": ndp // nx, "nx": nx, "ny": n // nc, "nc": nc}
    return jax.shard_map(
        functools.partial(on_device, cfg),
        mesh=mesh,
        in_specs=(
            P("dp", "seq", None),
            P("dp", "seq"),
            P(),
            P("dp", None),
            P(),
            P("dp", None),
            P(),
            P(),
        ),
        out_specs=(P("dp", "seq", None), P("dp", None, "seq"), P()),
        check_vma=False,
    )
```
